256 devices in a mesh: head: 4 (over y), chain: 4 (over x), seq: 16 (over z, core).
Axes of the slice: x: 4, y: 4, z: 8, core: 2. Of those that a mesh axis runs over, the one named last changes fastest.
Arguments:
- gate_signal: bfloat16 [8192, 4096], P(('chain', 'seq'), 'head'), may hold values from -6 to 6
- key: bfloat16 [8192, 4096], P(('chain', 'seq'), 'head'), may hold values from -0.017944336 to 0.017944336
- payload_vector: bfloat16 [8192, 4096], P(('chain', 'seq'), 'head'), may hold values from -6 to 6
- log_forgetting: float32 [8192, 4096], P(('chain', 'seq'), 'head'), may hold values from -1 to 0, as said below
- inline_erase_speed: bfloat16 [8192, 4096], P(('chain', 'seq'), 'head'), may hold values from 0.02 to 0.95
- erase_lookup_factor: float32 [64, 64], P('head'), may hold values from 0.08 to 3, as said below
- extra_gain: float32 [64, 64], P('head'), may hold values from -40 to 40
Outputs:
- head_output_rows: float32 [8192, 4096], P(('chain', 'seq'), 'head')
- shard_states: float32 [64, 64, 64, 64], P(('chain', 'seq'), 'head')
The draws below stay inside these ranges and needn't reach their ends.
Inputs may be any that keep to these rules, and one draw needn't show every extreme that they name: `log_forgetting`: entries are logarithms of decay factors, all negative. `erase_lookup_factor`: positive factors.
All inputs are finite; a program needn't handle non-finite values.
Results may differ from the reference program's by a relative error of at most 0.0003.
Values sent between devices are 32-bit elements; how exact they have to be, the bound alone decides.
A program may use at most 192 MiB of HBM per device.

```python
import math
import jax
import jax.numpy as jnp
from jax import lax

LANE_COUNT = 64
LANE_WIDTH = 64
T_DEV = 128
SHARDS = 64
PROMPT_TOKENS = 8192


def draw_log_forgetting(key, part):
    every_key_row = jax.random.split(key, 6)
    fast_share = 0.5
    fast_heads = jax.random.uniform(every_key_row[0], (LANE_COUNT,)) < fast_share
    fast_rate = jax.random.uniform(every_key_row[1], (LANE_COUNT, LANE_WIDTH), minval=1.0 / 50.0, maxval=1.0 / 30.0)
    slow_rate = math.log(10.0) / PROMPT_TOKENS * jnp.exp(jax.random.uniform(every_key_row[2], (LANE_COUNT, LANE_WIDTH), minval=math.log(0.05), maxval=math.log(0.4)))
    baseline_rate = jnp.where(fast_heads[:, None], fast_rate, slow_rate)
    approximate_output = jnp.exp(jax.random.uniform(every_key_row[3], (PROMPT_TOKENS, LANE_COUNT, LANE_WIDTH), minval=-0.7, maxval=0.7))
    spike_enabled = jax.random.uniform(every_key_row[4], (PROMPT_TOKENS, LANE_COUNT)) < 3.0 / PROMPT_TOKENS
    spike_magnitude = jnp.log(jax.random.uniform(every_key_row[5], (PROMPT_TOKENS, LANE_COUNT), minval=0.5, maxval=0.8))
    spike_contribution = jnp.where(spike_enabled, spike_magnitude, 0.0)
    final_output = -baseline_rate[None, :, :] * approximate_output + spike_contribution[:, :, None]
    return final_output.reshape(PROMPT_TOKENS, LANE_COUNT * LANE_WIDTH).astype(jnp.float32)


def kept_mask(key):
    return jax.random.uniform(jax.random.fold_in(key, 7001), (LANE_COUNT, LANE_WIDTH)) < 0.5


def draw_erase_lookup_factor(key, part):
    retained = kept_mask(key)
    every_key_row = jax.random.split(jax.random.fold_in(key, 7002), 2)
    small_gain = jnp.exp(jax.random.uniform(every_key_row[0], (LANE_COUNT, LANE_WIDTH), minval=math.log(0.08), maxval=math.log(0.25)))
    large_gain = jnp.exp(jax.random.uniform(every_key_row[1], (LANE_COUNT, LANE_WIDTH), minval=math.log(0.5), maxval=math.log(3.0)))
    return jnp.where(retained, small_gain, large_gain).astype(jnp.float32)


def draw_inline_erase_speed(key, part):
    retained = kept_mask(key)
    every_key_row = jax.random.split(jax.random.fold_in(key, 7003), 2)
    centres = jnp.where(retained, -7.0, jax.random.uniform(every_key_row[0], (LANE_COUNT, LANE_WIDTH), minval=-2.0, maxval=2.0))
    jitter = jnp.clip(jax.random.normal(every_key_row[1], (PROMPT_TOKENS, LANE_COUNT, LANE_WIDTH)), -4.0, 4.0)
    removal = 0.021 + 0.929 * jax.nn.sigmoid(centres[None, :, :] + jitter)
    return removal.reshape(PROMPT_TOKENS, LANE_COUNT * LANE_WIDTH).astype(jnp.bfloat16)


def shard_levels(stream_key, extent, cuts, least, high):
    loudness = 1.0
    for axis_at, blocks in cuts:
        draws = jax.random.uniform(jax.random.fold_in(jax.random.fold_in(stream_key, 6), axis_at), (blocks,), jnp.float32, least / len(cuts), high / len(cuts))
        loudness = loudness * jnp.repeat(jnp.exp(draws), extent[axis_at] // blocks).reshape((-1,) + (1,) * (len(extent) - 1 - axis_at))
    return loudness


def normal_values(own_key, shape, width, limit, cuts=(), held_as=jnp.bfloat16):
    factor_of = shard_levels(own_key, shape, cuts, -0.22, 0.18) if cuts else 1.0
    result = jax.random.normal(own_key, shape, jnp.float32) * width * factor_of
    return jnp.minimum(jnp.maximum(result, -limit), limit).astype(held_as)


def setup_inputs(seed: int = 0) -> dict:
    streams_of = jax.random.split(jax.random.key(seed), 8)
    gate_signal = normal_values(streams_of[0], (PROMPT_TOKENS, LANE_COUNT * LANE_WIDTH), 1.0, 6.0, ((0, 64), (1, 4)))
    key = normal_values(streams_of[1], (PROMPT_TOKENS, LANE_COUNT * LANE_WIDTH), 0.003, 0.017944336, ((0, 64), (1, 4)))
    payload_vector = normal_values(streams_of[2], (PROMPT_TOKENS, LANE_COUNT * LANE_WIDTH), 1.0, 6.0, ((0, 64), (1, 4)))
    log_forgetting = draw_log_forgetting(jax.random.fold_in(streams_of[7], 71), 0)
    inline_erase_speed = draw_inline_erase_speed(jax.random.fold_in(streams_of[7], 71), 0)
    erase_lookup_factor = draw_erase_lookup_factor(jax.random.fold_in(streams_of[7], 71), 0)
    extra_gain = normal_values(streams_of[6], (LANE_COUNT, LANE_WIDTH), 8.0, 40.0, ((0, 4),), jnp.float32)
    return {"gate_signal": gate_signal, "key": key, "payload_vector": payload_vector, "log_forgetting": log_forgetting, "inline_erase_speed": inline_erase_speed, "erase_lookup_factor": erase_lookup_factor, "extra_gain": extra_gain}


def reference(gate_signal, key, payload_vector, log_forgetting, inline_erase_speed, erase_lookup_factor, extra_gain):
    precise = lax.Precision.HIGHEST
    sequences = tuple((source.reshape(SHARDS, T_DEV, LANE_COUNT, LANE_WIDTH) for source in (gate_signal, key, payload_vector, log_forgetting, inline_erase_speed)))
    key_gains = erase_lookup_factor.astype(jnp.float32)
    extra_gain_factor = extra_gain.astype(jnp.float32)

    def token_step(carried, inputs):
        gate_signal_draws, lookup_vector_draws, payload_draws, log_data, rate_data = [source.astype(jnp.float32) for source in inputs]
        removal_key = lookup_vector_draws * key_gains
        removal_key = removal_key * lax.rsqrt(LANE_WIDTH * (lax.optimization_barrier(jnp.mean(removal_key * removal_key, axis=-1, keepdims=True)) + 1e-06))
        removal_dir = rate_data * removal_key
        read_out = jnp.einsum('hi,hij->hj', removal_key, carried, precision=precise)
        carried = jnp.exp(log_data)[:, :, None] * carried - removal_dir[:, :, None] * read_out[:, None, :] + lookup_vector_draws[:, :, None] * payload_draws[:, None, :]
        symbol_result_lines = jnp.einsum('hi,hij->hj', gate_signal_draws, carried, precision=precise)
        symbol_result_lines = symbol_result_lines + lax.optimization_barrier(jnp.sum(gate_signal_draws * extra_gain_factor * lookup_vector_draws, axis=-1, keepdims=True)) * payload_draws
        return (carried, symbol_result_lines)

    def shard_step(carried, inputs):
        carried, token_outs = lax.scan(token_step, carried, inputs)
        return (carried, (token_outs, carried))
    initial = jnp.zeros((LANE_COUNT, LANE_WIDTH, LANE_WIDTH), jnp.float32)
    state_end, (token_outs, shard_states) = lax.scan(shard_step, initial, sequences)
    return (token_outs.reshape(PROMPT_TOKENS, LANE_COUNT * LANE_WIDTH), shard_states)
```

```python
import functools

import jax
import jax.numpy as jnp
from jax import lax
from jax.experimental import pallas as pl
from jax.experimental.pallas import tpu as pltpu
from jax.sharding import PartitionSpec as P

MESH = pl.DeviceIdType.MESH
WIDTH = 64
PAIR = 2 * WIDTH
PAIRS_PER_STEP = 2
F32 = jnp.float32
BF16 = jnp.bfloat16


def halves(x):
    high = x.astype(BF16)
    return high, (x - high.astype(F32)).astype(BF16)


def thirds(x):
    high = x.astype(BF16)
    rest = x - high.astype(F32)
    mid = rest.astype(BF16)
    return high, mid, (rest - mid.astype(F32)).astype(BF16)


def dot(a, b):
    return jnp.dot(a, b, preferred_element_type=F32)


def dot_nt(a, b):
    return lax.dot_general(a, b, (((1,), (1,)), ((), ())), preferred_element_type=F32)


def lanes(*parts):
    return jnp.concatenate(parts, axis=1)


def rows(*parts):
    return jnp.concatenate(parts, axis=0)


def product(x, y):
    right = lanes(*y)
    both = dot(lanes(*x), rows(right, right))
    return both[:, :PAIR] + both[:, PAIR:]


def odd_rows(x, size):
    return rows(*[x[at : at + size] for at in range(size, x.shape[0], 2 * size)])


def spread_rows(x, size, count):
    blank = jnp.zeros((size, x.shape[1]), x.dtype)
    parts = []
    for at in range(0, count // 2, size):
        parts += [blank, x[at : at + size]]
    return rows(*parts)


def local_kernel(
    r_ref, k_ref, v_ref, w_ref, a_ref, factor_ref, gain_ref, own_ref, reach_ref, summ_ref
):
    tokens = r_ref.shape[0]
    half = tokens // 2
    row = lax.broadcasted_iota(jnp.int32, (tokens, tokens), 0)
    col = lax.broadcasted_iota(jnp.int32, (tokens, tokens), 1)
    strict = row > col
    incl = row >= col
    lane = lax.broadcasted_iota(jnp.int32, (tokens, PAIR), 1)
    first = lane < WIDTH
    signs = jnp.where(
        (row >= col) & (col >= half), 1.0, jnp.where((row < col) & (col < half), -1.0, 0.0)
    ).astype(BF16)
    row2 = lax.broadcasted_iota(jnp.int32, (2 * PAIR, PAIR), 0)
    col2 = lax.broadcasted_iota(jnp.int32, (2 * PAIR, PAIR), 1)
    same = jnp.where((row2 // WIDTH) % 2 == col2 // WIDTH, 1.0, 0.0).astype(BF16)
    srow = lax.broadcasted_iota(jnp.int32, (WIDTH, PAIR), 0)
    slane = lax.broadcasted_iota(jnp.int32, (WIDTH, PAIR), 1)
    diagonal = srow == slane % WIDTH
    sfirst = slane < WIDTH
    zero = jnp.zeros((), F32)

    pairs = range(PAIRS_PER_STEP)
    prepared = []
    for p in pairs:
        at = pl.ds(p * PAIR, PAIR)
        r = r_ref[:, at].astype(F32)
        k = k_ref[:, at].astype(F32)
        v = v_ref[:, at]
        log_w = w_ref[:, at]
        a = a_ref[:, at].astype(F32)
        removal = k * factor_ref[0, :, at]
        square = dot(lanes(*halves(removal * removal)), same)
        bonus = dot(lanes(*halves(r * gain_ref[0, :, at] * k)), same)
        kappa = removal * lax.rsqrt(square + 1e-06 * WIDTH)
        b = a * kappa
        cum = sum(dot(signs, part) for part in reversed(thirds(log_w)))
        start = cum[0:1] - log_w[0:1]
        last = cum[tokens - 1 : tokens]
        from_start = jnp.exp(-start)
        to_end = jnp.exp(last)
        whole = jnp.exp(last - start)
        fade = jnp.exp(cum)
        grow = jnp.exp(-cum)
        r_mid = r * fade
        kappa_mid = kappa * jnp.exp(cum - log_w)
        k_mid = k * grow
        b_mid = b * grow
        left = halves(rows(kappa_mid, r_mid))
        right = rows(b_mid, k_mid)
        ends = halves(jnp.transpose(lanes(k_mid * to_end, b_mid * -to_end)))
        swapped = pltpu.roll(kappa_mid * from_start, WIDTH, 1)
        reach = pltpu.roll(r_mid * from_start, WIDTH, 1)
        whole = pltpu.roll(jnp.broadcast_to(whole, (WIDTH, PAIR)), WIDTH, 1)
        prepared.append((v, left, halves(right), ends, swapped, reach, whole, bonus))

    heads = [(p, h) for p in pairs for h in range(2)]
    scores = []
    for p, h in heads:
        v, left, right, *_ = prepared[p]
        keep = (lax.broadcasted_iota(jnp.int32, (2 * tokens, PAIR), 1) < WIDTH) == (h == 0)
        high, low = [jnp.where(keep, part, jnp.zeros((), BF16)) for part in right]
        scores.append(dot_nt(lanes(*left), lanes(high, high)) + dot_nt(left[0], low))
    lower = [jnp.where(strict, s[:tokens, :tokens], zero) for s in scores]
    mix_key = [halves(jnp.where(strict, s[:tokens, tokens:], zero)) for s in scores]
    reads = [
        halves(
            lanes(
                jnp.where(incl, s[tokens:, tokens:], zero),
                jnp.where(incl, -s[tokens:, :tokens], zero),
            )
        )
        for s in scores
    ]
    values, wanted = [], []
    for i, (p, h) in enumerate(heads):
        v, swapped = prepared[p][0], prepared[p][4]
        mine = first == (h == 0)
        own_v = jnp.where(mine, v, jnp.zeros((), BF16))
        values.append(own_v)
        pushed = dot(lanes(*mix_key[i]), rows(own_v, own_v))
        wanted.append(pushed + jnp.where(mine, zero, swapped))

    eye = jnp.where(row == col, 1.0, 0.0)
    inverse = [eye - jnp.where(row // 2 == col // 2, l, zero) for l in lower]
    size = 2
    while size < tokens:
        inside = (row // (2 * size) == col // (2 * size)) & (row // size != col // size)
        edge = [jnp.where(inside, l, zero) for l in lower]
        parts = [halves(m) for m in inverse]
        if size < 16:
            step = [product(halves(e), m) for e, m in zip(edge, parts)]
            step = [product(m, halves(s)) for s, m in zip(step, parts)]
        else:
            step = [product(halves(odd_rows(e, size)), m) for e, m in zip(edge, parts)]
            step = [
                product(
                    [odd_rows(part, size) for part in m],
                    [spread_rows(part, size, tokens) for part in halves(s)],
                )
                for s, m in zip(step, parts)
            ]
            step = [spread_rows(s, size, tokens) for s in step]
        inverse = [m - s for m, s in zip(inverse, step)]
        size *= 2

    removed = [halves(product(halves(m), halves(w))) for m, w in zip(inverse, wanted)]
    outs = []
    for i, (p, h) in enumerate(heads):
        ends = prepared[p][3]
        cut = slice(h * WIDTH, (h + 1) * WIDTH)
        end_high, end_low = [
            lanes(e[cut, :], e[PAIR + h * WIDTH : PAIR + (h + 1) * WIDTH, :]) for e in ends
        ]
        stack = rows(reads[i][0], end_high, reads[i][1], end_low)
        right = rows(
            lanes(values[i], jnp.zeros_like(values[i])), lanes(*removed[i])
        )
        both = dot(stack, right)
        both = both[:, :PAIR] + both[:, PAIR:]
        count = tokens + WIDTH
        outs.append(both[:count] + both[count:])
    for p in pairs:
        at = pl.ds(p * PAIR, PAIR)
        v, _, _, _, _, reach, whole, bonus = prepared[p]
        one, two = outs[2 * p], outs[2 * p + 1]
        own_ref[:, at] = jnp.where(first, one[:tokens], two[:tokens]) + bonus * v.astype(F32)
        reach_ref[:, at] = reach + jnp.where(first, two[:tokens], one[:tokens])
        fade = jnp.where(diagonal, whole, zero)
        summ_ref[2 * p] = one[tokens:] + jnp.where(sfirst, zero, fade)
        summ_ref[2 * p + 1] = pltpu.roll(two[tokens:] + jnp.where(sfirst, fade, zero), WIDTH, 1)


def local_part(r, k, v, log_w, a, factor, gain):
    tokens, columns = r.shape
    heads = columns // WIDTH
    wide = PAIRS_PER_STEP * PAIR
    steps = columns // wide
    spec = pl.BlockSpec((tokens, wide), lambda i: (0, i))
    row_spec = pl.BlockSpec((1, 1, wide), lambda i: (i, 0, 0))
    return pl.pallas_call(
        local_kernel,
        grid=(steps,),
        in_specs=[spec] * 5 + [row_spec] * 2,
        out_specs=[
            spec,
            spec,
            pl.BlockSpec((2 * PAIRS_PER_STEP, WIDTH, PAIR), lambda i: (i, 0, 0)),
        ],
        out_shape=[
            jax.ShapeDtypeStruct((tokens, columns), F32),
            jax.ShapeDtypeStruct((tokens, columns), F32),
            jax.ShapeDtypeStruct((heads, WIDTH, PAIR), F32),
        ],
        name="local",
    )(r, k, v, log_w, a, factor.reshape(steps, 1, wide), gain.reshape(steps, 1, wide))


def advance(summary, state):
    pad = jnp.zeros((WIDTH, PAIR), F32)
    lane = lax.broadcasted_iota(jnp.int32, (WIDTH, PAIR), 1)
    moved = product(halves(summary), halves(rows(pad, state)))
    return moved + jnp.where(lane < WIDTH, summary, 0.0)


def prefix_kernel(
    chains, seqs, summ_ref, carry_ref, parts, totals, before, inbox, outbox,
    send_a, recv_a, send_b, recv_b, send_c, recv_c,
):
    chain = lax.axis_index("chain")
    seq = lax.axis_index("seq")
    barrier = pltpu.get_barrier_semaphore()

    def peer(step):
        return lax.rem(seq + step, seqs)

    def link(step):
        return lax.rem(chain + step, chains)

    def greet(step, _):
        pl.semaphore_signal(barrier, inc=1, device_id={"seq": peer(step)}, device_id_type=MESH)
        return 0

    lax.fori_loop(1, seqs, greet, 0)
    for step in range(1, chains):
        pl.semaphore_signal(barrier, inc=1, device_id={"chain": link(step)}, device_id_type=MESH)
    pl.semaphore_wait(barrier, seqs + chains - 2)

    def gather(step):
        return pltpu.make_async_remote_copy(
            src_ref=summ_ref.at[peer(step)],
            dst_ref=parts.at[seqs - step],
            send_sem=send_a.at[step],
            recv_sem=recv_a.at[seqs - step],
            device_id={"seq": peer(step)},
            device_id_type=MESH,
        )

    def start(step, _):
        gather(step).start()
        return 0

    lax.fori_loop(1, seqs, start, 0)
    parts[0] = summ_ref[seq]

    def arrived(step, _):
        gather(step).wait_recv()
        return 0

    lax.fori_loop(1, seqs, arrived, 0)
    row = lax.broadcasted_iota(jnp.int32, (WIDTH, PAIR), 0)
    lane = lax.broadcasted_iota(jnp.int32, (WIDTH, PAIR), 1)
    nothing = jnp.where(lane == row + WIDTH, 1.0, 0.0)

    def scan(shard, state):
        before[shard] = state
        return advance(parts[lax.rem(shard - seq + seqs, seqs)], state)

    total = lax.fori_loop(0, seqs, scan, nothing)
    totals[0] = total

    def pass_on(step):
        return pltpu.make_async_remote_copy(
            src_ref=totals.at[0],
            dst_ref=totals.at[chains - step],
            send_sem=send_b.at[step],
            recv_sem=recv_b.at[chains - step],
            device_id={"chain": link(step)},
            device_id_type=MESH,
        )

    for step in range(1, chains):
        pass_on(step).start()
    for step in range(1, chains):
        pass_on(step).wait_recv()
    state = nothing
    for place in range(chains - 1):
        there = totals[lax.rem(place - chain + chains, chains)]
        state = jnp.where(place < chain, advance(there, state), state)

    entry = halves(rows(jnp.zeros((WIDTH, PAIR), F32), state))

    def enter(shard, _):
        summary = before[shard]
        moved = product(halves(summary), entry) + summary
        outbox[lax.rem(shard - seq + seqs, seqs)] = lanes(
            moved[: WIDTH // 2, :WIDTH], moved[WIDTH // 2 :, :WIDTH]
        )
        return 0

    lax.fori_loop(0, seqs, enter, 0)

    def reply(step):
        return pltpu.make_async_remote_copy(
            src_ref=outbox.at[step],
            dst_ref=inbox.at[seq],
            send_sem=send_c.at[step],
            recv_sem=recv_c.at[seqs - step],
            device_id={"seq": peer(step)},
            device_id_type=MESH,
        )

    def start_reply(step, _):
        reply(step).start()
        return 0

    lax.fori_loop(1, seqs, start_reply, 0)
    inbox[seq] = outbox[0]

    def back(step, _):
        reply(step).wait_recv()
        return 0

    lax.fori_loop(1, seqs, back, 0)
    carry_ref[...] = inbox[...]

    def sent(step, _):
        gather(step).wait_send()
        reply(step).wait_send()
        return 0

    lax.fori_loop(1, seqs, sent, 0)
    for step in range(1, chains):
        pass_on(step).wait_send()


def prefix_part(summ, chains, seqs):
    heads = summ.shape[0]
    half = WIDTH // 2
    return pl.pallas_call(
        functools.partial(prefix_kernel, chains, seqs),
        in_specs=[pl.BlockSpec(memory_space=pltpu.VMEM)],
        out_specs=pl.BlockSpec(memory_space=pltpu.VMEM),
        out_shape=jax.ShapeDtypeStruct((heads, half, PAIR), F32),
        scratch_shapes=[
            pltpu.VMEM((seqs, WIDTH, PAIR), F32),
            pltpu.VMEM((chains, WIDTH, PAIR), F32),
            pltpu.VMEM((seqs, WIDTH, PAIR), F32),
            pltpu.VMEM((seqs, half, PAIR), F32),
            pltpu.VMEM((seqs, half, PAIR), F32),
            pltpu.SemaphoreType.DMA((seqs,)),
            pltpu.SemaphoreType.DMA((seqs,)),
            pltpu.SemaphoreType.DMA((chains,)),
            pltpu.SemaphoreType.DMA((chains,)),
            pltpu.SemaphoreType.DMA((seqs,)),
            pltpu.SemaphoreType.DMA((seqs,)),
        ],
        compiler_params=pltpu.CompilerParams(collective_id=0, has_side_effects=True),
        name="prefix",
    )(summ)


def apply_kernel(own_ref, reach_ref, summ_ref, carry_ref, out_ref, state_ref):
    zero = jnp.zeros((WIDTH, WIDTH), F32)
    for p in range(PAIRS_PER_STEP):
        at = pl.ds(p * PAIR, PAIR)
        one, two = [
            rows(carry_ref[2 * p + h][:, :WIDTH], carry_ref[2 * p + h][:, WIDTH:]) for h in range(2)
        ]
        entry = halves(rows(lanes(zero, two), lanes(one, zero)))
        out_ref[:, at] = own_ref[:, at] + product(halves(reach_ref[:, at]), entry)
        for h, mine in enumerate((one, two)):
            summary = summ_ref[2 * p + h]
            right = halves(rows(zero, mine))
            wide = lanes(*right)
            both = dot(lanes(*halves(summary)), rows(wide, wide))
            state_ref[0, 2 * p + h] = (
                both[:, :WIDTH] + both[:, WIDTH:] + summary[:, :WIDTH]
            )


def apply_part(own, reach, summ, carry):
    tokens, columns = own.shape
    heads = summ.shape[0]
    wide = PAIRS_PER_STEP * PAIR
    per = 2 * PAIRS_PER_STEP
    spec = pl.BlockSpec((tokens, wide), lambda i: (0, i))
    return pl.pallas_call(
        apply_kernel,
        grid=(columns // wide,),
        in_specs=[
            spec,
            spec,
            pl.BlockSpec((per, WIDTH, PAIR), lambda i: (i, 0, 0)),
            pl.BlockSpec((per, WIDTH // 2, PAIR), lambda i: (i, 0, 0)),
        ],
        out_specs=[spec, pl.BlockSpec((1, per, WIDTH, WIDTH), lambda i: (0, i, 0, 0))],
        out_shape=[
            jax.ShapeDtypeStruct((tokens, columns), F32),
            jax.ShapeDtypeStruct((1, heads, WIDTH, WIDTH), F32),
        ],
        name="apply",
    )(own, reach, summ, carry)


def solution(mesh):
    chains, seqs = mesh.shape["chain"], mesh.shape["seq"]

    def body(r, k, v, log_w, a, factor, gain):
        own, reach, summ = local_part(r, k, v, log_w, a, factor, gain)
        carry = prefix_part(summ, chains, seqs)
        return apply_part(own, reach, summ, carry)

    wide = P(("chain", "seq"), "head")
    return jax.shard_map(
        body,
        mesh=mesh,
        in_specs=(wide,) * 5 + (P("head", None),) * 2,
        out_specs=(wide, P(("chain", "seq"), "head", None, None)),
        check_vma=False,
    )
```

```python
import functools

import jax
import jax.numpy as jnp
from jax import lax
from jax.experimental import pallas as pl
from jax.experimental.pallas import tpu as pltpu
from jax.sharding import PartitionSpec as P

MESH = pl.DeviceIdType.MESH
WIDTH = 64
PAIR = 2 * WIDTH
PAIRS_PER_STEP = 2
HEADS_PER_STEP = 2 * PAIRS_PER_STEP
F32 = jnp.float32
BF16 = jnp.bfloat16


def halves(x):
    high = x.astype(BF16)
    return high, (x - high.astype(F32)).astype(BF16)


def thirds(x):
    high = x.astype(BF16)
    rest = x - high.astype(F32)
    mid = rest.astype(BF16)
    return high, mid, (rest - mid.astype(F32)).astype(BF16)


def dot(a, b):
    return jnp.dot(a, b, preferred_element_type=F32)


def dot_nt(a, b):
    return lax.dot_general(a, b, (((1,), (1,)), ((), ())), preferred_element_type=F32)


def lanes(*parts):
    return jnp.concatenate(parts, axis=1)


def rows(*parts):
    return jnp.concatenate(parts, axis=0)


def product(x, y):
    right = lanes(*y)
    both = dot(lanes(*x), rows(right, right))
    return both[:, :PAIR] + both[:, PAIR:]


def odd_rows(x, size):
    return rows(*[x[at : at + size] for at in range(size, x.shape[0], 2 * size)])


def spread_rows(x, size, count):
    blank = jnp.zeros((size, x.shape[1]), x.dtype)
    parts = []
    for at in range(0, count // 2, size):
        parts += [blank, x[at : at + size]]
    return rows(*parts)


def advance(summary, state):
    pad = jnp.zeros((WIDTH, PAIR), F32)
    lane = lax.broadcasted_iota(jnp.int32, (WIDTH, PAIR), 1)
    moved = product(halves(summary), halves(rows(pad, state)))
    return moved + jnp.where(lane < WIDTH, summary, 0.0)


def side_by_side(ref, head):
    return lanes(ref[pl.ds(head, 1), :], ref[pl.ds(head + 1, 1), :])


def local_step(
    group, r_ref, k_ref, v_ref, w_ref, a_ref, factor_ref, gain_ref,
    own, reach, maps, sums, reads, rights, summ,
):
    tokens = r_ref.shape[0]
    half = tokens // 2
    row = lax.broadcasted_iota(jnp.int32, (tokens, tokens), 0)
    col = lax.broadcasted_iota(jnp.int32, (tokens, tokens), 1)
    strict = row > col
    incl = row >= col
    lane = lax.broadcasted_iota(jnp.int32, (tokens, PAIR), 1)
    first = lane < WIDTH
    signs = jnp.where(
        (row >= col) & (col >= half), 1.0, jnp.where((row < col) & (col < half), -1.0, 0.0)
    ).astype(BF16)
    row2 = lax.broadcasted_iota(jnp.int32, (2 * PAIR, PAIR), 0)
    col2 = lax.broadcasted_iota(jnp.int32, (2 * PAIR, PAIR), 1)
    same = jnp.where((row2 // WIDTH) % 2 == col2 // WIDTH, 1.0, 0.0).astype(BF16)
    srow = lax.broadcasted_iota(jnp.int32, (WIDTH, PAIR), 0)
    slane = lax.broadcasted_iota(jnp.int32, (WIDTH, PAIR), 1)
    diagonal = srow == slane % WIDTH
    sfirst = slane < WIDTH
    zero = jnp.zeros((), F32)

    pairs = range(PAIRS_PER_STEP)
    prepared = []
    for p in pairs:
        pair = group * PAIRS_PER_STEP + p
        at = pl.ds(pl.multiple_of(pair * PAIR, PAIR), PAIR)
        r = r_ref[:, at].astype(F32)
        k = k_ref[:, at].astype(F32)
        v = v_ref[:, at]
        log_w = w_ref[:, at]
        a = a_ref[:, at].astype(F32)
        removal = k * side_by_side(factor_ref, 2 * pair)
        square = dot(lanes(*halves(removal * removal)), same)
        bonus = dot(lanes(*halves(r * side_by_side(gain_ref, 2 * pair) * k)), same)
        own[:, at] = bonus * v.astype(F32)
        kappa = removal * lax.rsqrt(square + 1e-06 * WIDTH)
        b = a * kappa
        cum = sum(dot(signs, part) for part in reversed(thirds(log_w)))
        start = cum[0:1] - log_w[0:1]
        last = cum[tokens - 1 : tokens]
        from_start = jnp.exp(-start)
        to_end = jnp.exp(last)
        whole = jnp.exp(last - start)
        fade = jnp.exp(cum)
        grow = jnp.exp(-cum)
        r_mid = r * fade
        kappa_mid = kappa * jnp.exp(cum - log_w)
        k_mid = k * grow
        b_mid = b * grow
        left = halves(rows(kappa_mid, r_mid))
        right = rows(b_mid, k_mid)
        ends = halves(jnp.transpose(lanes(k_mid * to_end, b_mid * -to_end)))
        swapped = pltpu.roll(kappa_mid * from_start, WIDTH, 1)
        reach[:, at] = pltpu.roll(r_mid * from_start, WIDTH, 1)
        whole = pltpu.roll(jnp.broadcast_to(whole, (WIDTH, PAIR)), WIDTH, 1)
        prepared.append((v, left, halves(right), ends, swapped, whole))

    heads = [(p, h) for p in pairs for h in range(2)]
    scores = []
    for p, h in heads:
        v, left, right, *_ = prepared[p]
        keep = (lax.broadcasted_iota(jnp.int32, (2 * tokens, PAIR), 1) < WIDTH) == (h == 0)
        high, low = [jnp.where(keep, part, jnp.zeros((), BF16)) for part in right]
        scores.append(dot_nt(lanes(*left), lanes(high, high)) + dot_nt(left[0], low))
    lower = [jnp.where(strict, s[:tokens, :tokens], zero) for s in scores]
    mix_key = [halves(jnp.where(strict, s[:tokens, tokens:], zero)) for s in scores]
    for i, s in enumerate(scores):
        high, low = halves(
            lanes(
                jnp.where(incl, s[tokens:, tokens:], zero),
                jnp.where(incl, -s[tokens:, :tokens], zero),
            )
        )
        reads[group * HEADS_PER_STEP + i] = rows(high, low)
    values, wanted = [], []
    for i, (p, h) in enumerate(heads):
        v, swapped = prepared[p][0], prepared[p][4]
        mine = first == (h == 0)
        own_v = jnp.where(mine, v, jnp.zeros((), BF16))
        values.append(own_v)
        pushed = dot(lanes(*mix_key[i]), rows(own_v, own_v))
        wanted.append(pushed + jnp.where(mine, zero, swapped))

    eye = jnp.where(row == col, 1.0, 0.0)
    inverse = [eye - jnp.where(row // 2 == col // 2, l, zero) for l in lower]
    size = 2
    while size < tokens:
        inside = (row // (2 * size) == col // (2 * size)) & (row // size != col // size)
        edge = [jnp.where(inside, l, zero) for l in lower]
        parts = [halves(m) for m in inverse]
        if size < 16:
            step = [product(halves(e), m) for e, m in zip(edge, parts)]
            step = [product(m, halves(s)) for s, m in zip(step, parts)]
        else:
            step = [product(halves(odd_rows(e, size)), m) for e, m in zip(edge, parts)]
            step = [
                product(
                    [odd_rows(part, size) for part in m],
                    [spread_rows(part, size, tokens) for part in halves(s)],
                )
                for s, m in zip(step, parts)
            ]
            step = [spread_rows(s, size, tokens) for s in step]
        inverse = [m - s for m, s in zip(inverse, step)]
        size *= 2

    removed = [halves(product(halves(m), halves(w))) for m, w in zip(inverse, wanted)]
    outs = []
    for i, (p, h) in enumerate(heads):
        ends = prepared[p][3]
        cut = slice(h * WIDTH, (h + 1) * WIDTH)
        stack = rows(
            *[lanes(e[cut, :], e[PAIR + h * WIDTH : PAIR + (h + 1) * WIDTH, :]) for e in ends]
        )
        right = rows(lanes(values[i], jnp.zeros_like(values[i])), lanes(*removed[i]))
        rights[group * HEADS_PER_STEP + i] = right
        both = dot(stack, right)
        both = both[:, :PAIR] + both[:, PAIR:]
        outs.append(both[:WIDTH] + both[WIDTH:])
    for p in pairs:
        pair = group * PAIRS_PER_STEP + p
        fade = jnp.where(diagonal, prepared[p][5], zero)
        one = outs[2 * p] + jnp.where(sfirst, zero, fade)
        two = outs[2 * p + 1] + jnp.where(sfirst, fade, zero)
        summ[2 * pair] = one
        summ[2 * pair + 1] = pltpu.roll(two, WIDTH, 1)
        maps[pair] = jnp.where(sfirst, two, one)
        sums[pair] = jnp.where(sfirst, one, two)


def read_step(group, own, reach, reads, rights):
    tokens = own.shape[0]
    first = lax.broadcasted_iota(jnp.int32, (tokens, PAIR), 1) < WIDTH
    outs = []
    for i in range(HEADS_PER_STEP):
        head = group * HEADS_PER_STEP + i
        both = dot(reads[head], rights[head])
        both = both[:, :PAIR] + both[:, PAIR:]
        outs.append(both[:tokens] + both[tokens:])
    for p in range(PAIRS_PER_STEP):
        at = pl.ds(pl.multiple_of((group * PAIRS_PER_STEP + p) * PAIR, PAIR), PAIR)
        one, two = outs[2 * p], outs[2 * p + 1]
        own[:, at] += jnp.where(first, one, two)
        reach[:, at] += jnp.where(first, two, one)


def enter_step(pair, own, reach, maps, sums, inbox, out_ref, state_ref):
    tokens = own.shape[0]
    zero = jnp.zeros((WIDTH, WIDTH), F32)
    at = pl.ds(pl.multiple_of(pair * PAIR, PAIR), PAIR)
    one, two = [
        rows(inbox[2 * pair + h][:, :WIDTH], inbox[2 * pair + h][:, WIDTH:]) for h in range(2)
    ]
    entry = halves(rows(lanes(zero, two), lanes(one, zero)))
    moved = product(halves(rows(reach[:, at], maps[pair])), entry)
    out_ref[:, at] = own[:, at] + moved[:tokens]
    after = sums[pair] + moved[tokens:]
    state_ref[0, 2 * pair] = after[:, :WIDTH]
    state_ref[0, 2 * pair + 1] = after[:, WIDTH:]


def kernel(
    chains, seqs, r_ref, k_ref, v_ref, w_ref, a_ref, factor_ref, gain_ref, out_ref, state_ref,
    own, reach, maps, sums, reads, rights, summ, parts, totals, inbox, outbox,
    send_a, recv_a, send_b, recv_b, send_c, recv_c,
):
    chain = lax.axis_index("chain")
    seq = lax.axis_index("seq")
    barrier = pltpu.get_barrier_semaphore()

    def peer(step):
        return lax.rem(seq + step, seqs)

    def link(step):
        return lax.rem(chain + step, chains)

    for step in range(1, seqs):
        pl.semaphore_signal(barrier, inc=1, device_id={"seq": peer(step)}, device_id_type=MESH)
    for step in range(1, chains):
        pl.semaphore_signal(barrier, inc=1, device_id={"chain": link(step)}, device_id_type=MESH)

    def gather(head, source):
        return pltpu.make_async_remote_copy(
            src_ref=summ.at[head],
            dst_ref=parts.at[source],
            send_sem=send_a.at[head],
            recv_sem=recv_a.at[source],
            device_id={"seq": head},
            device_id_type=MESH,
        )

    groups = seqs // HEADS_PER_STEP

    def local(step, _):
        group = lax.rem(seq // HEADS_PER_STEP + step + 1, groups)
        local_step(
            group, r_ref, k_ref, v_ref, w_ref, a_ref, factor_ref, gain_ref,
            own, reach, maps, sums, reads, rights, summ,
        )

        @pl.when(step == 0)
        def _():
            pl.semaphore_wait(barrier, seqs + chains - 2)

        for i in range(HEADS_PER_STEP):
            head = group * HEADS_PER_STEP + i

            @pl.when(head != seq)
            def _():
                gather(head, seq).start()

        return 0

    lax.fori_loop(0, groups, local, 0)
    parts[seq] = summ[seq]

    def read(group, _):
        read_step(group, own, reach, reads, rights)
        return 0

    lax.fori_loop(0, groups, read, 0)

    for source in range(seqs):

        @pl.when(source != seq)
        def _():
            gather(source, source).wait_recv()

    levels = [[parts[shard] for shard in range(seqs)]]
    while len(levels[-1]) > 1:
        below = levels[-1]
        levels.append([advance(below[i + 1], below[i]) for i in range(0, len(below), 2)])
    totals[chain] = levels[-1][0]

    def pass_on(step):
        return pltpu.make_async_remote_copy(
            src_ref=totals.at[chain],
            dst_ref=totals.at[chain],
            send_sem=send_b.at[step],
            recv_sem=recv_b.at[chains - step],
            device_id={"chain": link(step)},
            device_id_type=MESH,
        )

    for step in range(1, chains):
        pass_on(step).start()

    row = lax.broadcasted_iota(jnp.int32, (WIDTH, PAIR), 0)
    lane = lax.broadcasted_iota(jnp.int32, (WIDTH, PAIR), 1)
    nothing = jnp.where(lane == row + WIDTH, 1.0, 0.0)
    before = [None]
    for level in reversed(levels[:-1]):
        spread = []
        for i, state in enumerate(before):
            here = level[2 * i]
            spread += [state, here if state is None else advance(here, state)]
        before = spread
    before[0] = nothing

    for step in range(1, chains):
        pass_on(step).wait_recv()
    state = jnp.where(chain > 0, totals[0], 0.0)
    for place in range(1, chains - 1):
        state = jnp.where(place < chain, advance(totals[place], state), state)
    lane = lax.broadcasted_iota(jnp.int32, (WIDTH, PAIR), 1)
    state = jnp.where(lane < WIDTH, state, 0.0)

    entry = halves(rows(jnp.zeros((WIDTH, PAIR), F32), state))
    for shard in range(seqs):
        moved = product(halves(before[shard]), entry) + before[shard]
        outbox[shard] = lanes(moved[: WIDTH // 2, :WIDTH], moved[WIDTH // 2 :, :WIDTH])

    def reply(step):
        return pltpu.make_async_remote_copy(
            src_ref=outbox.at[peer(step)],
            dst_ref=inbox.at[seq],
            send_sem=send_c.at[step],
            recv_sem=recv_c.at[seqs - step],
            device_id={"seq": peer(step)},
            device_id_type=MESH,
        )

    def start_reply(step, _):
        reply(step).start()
        return 0

    lax.fori_loop(1, seqs, start_reply, 0)
    inbox[seq] = outbox[seq]

    for step in range(1, seqs):
        reply(step).wait_recv()

    def enter(pair, _):
        enter_step(pair, own, reach, maps, sums, inbox, out_ref, state_ref)
        return 0

    lax.fori_loop(0, seqs // 2, enter, 0)

    for step in range(1, seqs):
        reply(step).wait_send()
    for step in range(1, chains):
        pass_on(step).wait_send()
    for head in range(seqs):

        @pl.when(head != seq)
        def _():
            gather(head, seq).wait_send()


def solution(mesh):
    chains, seqs = mesh.shape["chain"], mesh.shape["seq"]

    def body(r, k, v, log_w, a, factor, gain):
        tokens, columns = r.shape
        heads = columns // WIDTH
        half = WIDTH // 2
        vmem = pl.BlockSpec(memory_space=pltpu.VMEM)
        return pl.pallas_call(
            functools.partial(kernel, chains, seqs),
            in_specs=[vmem] * 7,
            out_specs=[vmem] * 2,
            out_shape=[
                jax.ShapeDtypeStruct((tokens, columns), F32),
                jax.ShapeDtypeStruct((1, heads, WIDTH, WIDTH), F32),
            ],
            scratch_shapes=[
                pltpu.VMEM((tokens, columns), F32),
                pltpu.VMEM((tokens, columns), F32),
                pltpu.VMEM((heads // 2, WIDTH, PAIR), F32),
                pltpu.VMEM((heads // 2, WIDTH, PAIR), F32),
                pltpu.VMEM((heads, 2 * tokens, 2 * tokens), BF16),
                pltpu.VMEM((heads, 2 * tokens, 2 * PAIR), BF16),
                pltpu.VMEM((heads, WIDTH, PAIR), F32),
                pltpu.VMEM((seqs, WIDTH, PAIR), F32),
                pltpu.VMEM((chains, WIDTH, PAIR), F32),
                pltpu.VMEM((heads, half, PAIR), F32),
                pltpu.VMEM((seqs, half, PAIR), F32),
                pltpu.SemaphoreType.DMA((seqs,)),
                pltpu.SemaphoreType.DMA((seqs,)),
                pltpu.SemaphoreType.DMA((chains,)),
                pltpu.SemaphoreType.DMA((chains,)),
                pltpu.SemaphoreType.DMA((seqs,)),
                pltpu.SemaphoreType.DMA((seqs,)),
            ],
            compiler_params=pltpu.CompilerParams(collective_id=0, has_side_effects=True),
            name="mix",
        )(r, k, v, log_w, a, factor, gain)

    wide = P(("chain", "seq"), "head")
    return jax.shard_map(
        body,
        mesh=mesh,
        in_specs=(wide,) * 5 + (P("head", None),) * 2,
        out_specs=(wide, P(("chain", "seq"), "head", None, None)),
        check_vma=False,
    )
```

```python
import functools

import jax
import jax.numpy as jnp
from jax import lax
from jax.experimental import pallas as pl
from jax.experimental.pallas import tpu as pltpu
from jax.sharding import PartitionSpec as P

MESH = pl.DeviceIdType.MESH
WIDTH = 64
PAIR = 2 * WIDTH
VMEM_LIMIT = 40 * 1024 * 1024
F32 = jnp.float32
BF16 = jnp.bfloat16


def halves(x):
    high = x.astype(BF16)
    return high, (x - high.astype(F32)).astype(BF16)


def thirds(x):
    high = x.astype(BF16)
    rest = x - high.astype(F32)
    mid = rest.astype(BF16)
    return high, mid, (rest - mid.astype(F32)).astype(BF16)


def dot(a, b):
    return jnp.dot(a, b, preferred_element_type=F32)


def dot_nt(a, b):
    return lax.dot_general(a, b, (((1,), (1,)), ((), ())), preferred_element_type=F32)


def lanes(*parts):
    return jnp.concatenate(parts, axis=1)


def rows(*parts):
    return jnp.concatenate(parts, axis=0)


def product(x, y):
    right = lanes(*y)
    both = dot(lanes(*x), rows(right, right))
    return both[:, :PAIR] + both[:, PAIR:]


def odd_rows(x, size):
    return rows(*[x[at : at + size] for at in range(size, x.shape[0], 2 * size)])


def spread_rows(x, size, count):
    blank = jnp.zeros((size, x.shape[1]), x.dtype)
    parts = []
    for at in range(0, count // 2, size):
        parts += [blank, x[at : at + size]]
    return rows(*parts)


def advance(summary, state):
    pad = jnp.zeros((WIDTH, PAIR), F32)
    lane = lax.broadcasted_iota(jnp.int32, (WIDTH, PAIR), 1)
    moved = product(halves(summary), halves(rows(pad, state)))
    return moved + jnp.where(lane < WIDTH, summary, 0.0)


def side_by_side(ref, head):
    return lanes(ref[head : head + 1, :], ref[head + 1 : head + 2, :])


def local_step(
    r_ref, k_ref, v_ref, w_ref, a_ref, factor_ref, gain_ref,
    own, reach, maps, sums, reads, rights, summ, masks,
):
    tokens = r_ref.shape[0]
    half = tokens // 2
    row = lax.broadcasted_iota(jnp.int32, (tokens, tokens), 0)
    col = lax.broadcasted_iota(jnp.int32, (tokens, tokens), 1)
    strict = row > col
    incl = row >= col
    lane = lax.broadcasted_iota(jnp.int32, (tokens, PAIR), 1)
    first = lane < WIDTH
    signs = jnp.where(
        (row >= col) & (col >= half), 1.0, jnp.where((row < col) & (col < half), -1.0, 0.0)
    ).astype(BF16)
    row2 = lax.broadcasted_iota(jnp.int32, (2 * PAIR, PAIR), 0)
    col2 = lax.broadcasted_iota(jnp.int32, (2 * PAIR, PAIR), 1)
    same = jnp.where((row2 // WIDTH) % 2 == col2 // WIDTH, 1.0, 0.0).astype(BF16)
    srow = lax.broadcasted_iota(jnp.int32, (WIDTH, PAIR), 0)
    slane = lax.broadcasted_iota(jnp.int32, (WIDTH, PAIR), 1)
    diagonal = srow == slane % WIDTH
    sfirst = slane < WIDTH
    zero = jnp.zeros((), F32)

    pairs = range(maps.shape[0])
    prepared = []
    for p in pairs:
        at = pl.ds(p * PAIR, PAIR)
        r = r_ref[:, at].astype(F32)
        k = k_ref[:, at].astype(F32)
        v = v_ref[:, at]
        log_w = w_ref[:, at]
        a = a_ref[:, at].astype(F32)
        removal = k * side_by_side(factor_ref, 2 * p)
        square = dot(lanes(*halves(removal * removal)), same)
        bonus = dot(lanes(*halves(r * side_by_side(gain_ref, 2 * p) * k)), same)
        own[:, at] = bonus * v.astype(F32)
        kappa = removal * lax.rsqrt(square + 1e-06 * WIDTH)
        b = a * kappa
        cum = sum(dot(signs, part) for part in reversed(thirds(log_w)))
        start = cum[0:1] - log_w[0:1]
        last = cum[tokens - 1 : tokens]
        from_start = jnp.exp(-start)
        to_end = jnp.exp(last)
        whole = jnp.exp(last - start)
        fade = jnp.exp(cum)
        grow = jnp.exp(-cum)
        r_mid = r * fade
        kappa_mid = kappa * jnp.exp(cum - log_w)
        k_mid = k * grow
        b_mid = b * grow
        left = halves(rows(kappa_mid, r_mid))
        right = rows(b_mid, k_mid)
        ends = halves(jnp.transpose(lanes(k_mid * to_end, b_mid * -to_end)))
        swapped = pltpu.roll(kappa_mid * from_start, WIDTH, 1)
        reach[:, at] = pltpu.roll(r_mid * from_start, WIDTH, 1)
        whole = pltpu.roll(jnp.broadcast_to(whole, (WIDTH, PAIR)), WIDTH, 1)
        prepared.append((v, left, halves(right), ends, swapped, whole))

    heads = [(p, h) for p in pairs for h in range(2)]
    scores = []
    for p, h in heads:
        v, left, right, *_ = prepared[p]
        keep = (lax.broadcasted_iota(jnp.int32, (2 * tokens, PAIR), 1) < WIDTH) == (h == 0)
        high, low = [jnp.where(keep, part, jnp.zeros((), BF16)) for part in right]
        scores.append(dot_nt(lanes(*left), lanes(high, high)) + dot_nt(left[0], low))
    lower = [jnp.where(strict, s[:tokens, :tokens], zero) for s in scores]
    mix_key = [halves(jnp.where(strict, s[:tokens, tokens:], zero)) for s in scores]
    for i, s in enumerate(scores):
        high, low = halves(
            lanes(
                jnp.where(incl, s[tokens:, tokens:], zero),
                jnp.where(incl, -s[tokens:, :tokens], zero),
            )
        )
        reads[i] = rows(high, low)
    values, wanted = [], []
    for i, (p, h) in enumerate(heads):
        v, swapped = prepared[p][0], prepared[p][4]
        mine = first == (h == 0)
        own_v = jnp.where(mine, v, jnp.zeros((), BF16))
        values.append(own_v)
        pushed = dot(lanes(*mix_key[i]), rows(own_v, own_v))
        wanted.append(pushed + jnp.where(mine, zero, swapped))

    lower = [halves(l) for l in lower]
    eye = jnp.where(row == col, 1.0, 0.0).astype(BF16)
    inverse = [(eye - high * masks[0], -low * masks[0]) for high, low in lower]
    size, level = 2, 1
    while size < tokens:
        mask = masks[level]
        edge = [(high * mask, low * mask) for high, low in lower]
        if size < 16:
            step = [product(e, m) for e, m in zip(edge, inverse)]
            step = [halves(product(m, halves(s))) for s, m in zip(step, inverse)]
        else:
            step = [
                product([odd_rows(part, size) for part in e], m) for e, m in zip(edge, inverse)
            ]
            step = [
                halves(
                    product(
                        [odd_rows(part, size) for part in m],
                        [spread_rows(part, size, tokens) for part in halves(s)],
                    )
                )
                for s, m in zip(step, inverse)
            ]
            step = [[spread_rows(part, size, tokens) for part in s] for s in step]
        inverse = [(m[0] - s[0], m[1] - s[1]) for m, s in zip(inverse, step)]
        size, level = 2 * size, level + 1

    removed = [halves(product(m, halves(w))) for m, w in zip(inverse, wanted)]
    outs = []
    for i, (p, h) in enumerate(heads):
        ends = prepared[p][3]
        cut = slice(h * WIDTH, (h + 1) * WIDTH)
        stack = rows(
            *[lanes(e[cut, :], e[PAIR + h * WIDTH : PAIR + (h + 1) * WIDTH, :]) for e in ends]
        )
        right = rows(lanes(values[i], jnp.zeros_like(values[i])), lanes(*removed[i]))
        rights[i] = right
        both = dot(stack, right)
        both = both[:, :PAIR] + both[:, PAIR:]
        outs.append(both[:WIDTH] + both[WIDTH:])
    for p in pairs:
        fade = jnp.where(diagonal, prepared[p][5], zero)
        one = outs[2 * p] + jnp.where(sfirst, zero, fade)
        two = outs[2 * p + 1] + jnp.where(sfirst, fade, zero)
        summ[0, p] = one
        summ[1, p] = pltpu.roll(two, WIDTH, 1)
        maps[p] = jnp.where(sfirst, two, one)
        sums[p] = jnp.where(sfirst, one, two)


def read_step(group, count, own, reach, reads, rights):
    tokens = own.shape[0]
    first = lax.broadcasted_iota(jnp.int32, (tokens, PAIR), 1) < WIDTH
    outs = []
    for i in range(2 * count):
        head = group * 2 * count + i
        both = dot(reads[head], rights[head])
        both = both[:, :PAIR] + both[:, PAIR:]
        outs.append(both[:tokens] + both[tokens:])
    for p in range(count):
        at = pl.ds(pl.multiple_of((group * count + p) * PAIR, PAIR), PAIR)
        one, two = outs[2 * p], outs[2 * p + 1]
        own[:, at] += jnp.where(first, one, two)
        reach[:, at] += jnp.where(first, two, one)


def fold_step(pair, own, reach, maps, sums, first, second):
    tokens = own.shape[0]
    low = lax.broadcasted_iota(jnp.int32, (WIDTH, PAIR), 1) < WIDTH
    at = pl.ds(pl.multiple_of(pair * PAIR, PAIR), PAIR)
    one, two = first[pair], pltpu.roll(second[pair], WIDTH, 1)
    right = rows(
        lanes(jnp.where(low, two, 0.0), jnp.where(low, 0.0, two)),
        lanes(jnp.where(low, 0.0, one), jnp.where(low, one, 0.0)),
    )
    high, rest = halves(right)
    left = halves(rows(reach[:, at], maps[pair]))
    moved = dot(lanes(*left), rows(high, high)) + dot(left[0], rest)
    reach[:, at] = moved[:tokens, :PAIR]
    own[:, at] += moved[:tokens, PAIR:]
    maps[pair] = moved[tokens:, :PAIR]
    sums[pair] += moved[tokens:, PAIR:]


def enter_step(pair, own, reach, maps, sums, inbox, out_ref, state_ref):
    tokens = own.shape[0]
    zero = jnp.zeros((WIDTH, WIDTH), F32)
    at = pl.ds(pl.multiple_of(pair * PAIR, PAIR), PAIR)
    one, two = [
        rows(inbox[h, pair][:, :WIDTH], inbox[h, pair][:, WIDTH:]) for h in range(2)
    ]
    entry = halves(rows(lanes(zero, two), lanes(one, zero)))
    moved = product(halves(rows(reach[:, at], maps[pair])), entry)
    out_ref[:, at] = own[:, at] + moved[:tokens]
    after = sums[pair] + moved[tokens:]
    state_ref[0, 2 * pair] = after[:, :WIDTH]
    state_ref[0, 2 * pair + 1] = after[:, WIDTH:]


def kernel(
    chains, chips, r_in, k_in, v_in, w_in, a_in, factor_in, gain_in, out_ref, state_ref,
    r_ref, k_ref, v_ref, w_ref, a_ref, factor_ref, gain_ref, load, own, reach, maps, sums, reads, rights, summ, masks, both, other, joined, parts, starts, totals,
    inbox, outbox, send_m, recv_m, send_a, recv_a, send_b, recv_b, send_c, recv_c, send_f, recv_f,
):
    sources = (factor_in, gain_in, w_in, k_in, a_in, r_in, v_in)
    targets = (factor_ref, gain_ref, w_ref, k_ref, a_ref, r_ref, v_ref)
    loads = [
        pltpu.make_async_copy(source, target, load.at[i])
        for i, (source, target) in enumerate(zip(sources, targets))
    ]
    for copy in loads:
        copy.start()
    chain = lax.axis_index("chain")
    seq = lax.axis_index("seq")
    core = lax.rem(seq, 2)
    chip = seq // 2
    partner = {"seq": seq + 1 - 2 * core}
    barrier = pltpu.get_barrier_semaphore()
    ways = sorted(range(1, chips), key=lambda way: -min(way, chips - way))

    def there(way):
        return lax.rem(chip + way, chips)

    def device(way):
        return {"seq": 2 * there(way) + core}

    def greet(device_id):
        pl.semaphore_signal(barrier, inc=1, device_id=device_id, device_id_type=MESH)

    totals[...] = jnp.zeros_like(totals)
    greet(partner)
    for way in ways:
        greet(device(way))
    for step in range(1, chains):
        greet({"chain": lax.rem(chain + step, chains)})
    row = lax.broadcasted_iota(jnp.int32, masks.shape[1:], 0)
    col = lax.broadcasted_iota(jnp.int32, masks.shape[1:], 1)
    for level in range(masks.shape[0]):
        size = 1 << level
        inside = (row // (2 * size) == col // (2 * size)) & (row // size > col // size)
        masks[level] = jnp.where(inside, 1.0, 0.0).astype(BF16)

    for copy in loads:
        copy.wait()
    local_step(
        r_ref, k_ref, v_ref, w_ref, a_ref, factor_ref, gain_ref,
        own, reach, maps, sums, reads, rights, summ, masks,
    )
    pl.semaphore_wait(barrier, chips + chains - 1)

    def swap(slot, source, target):
        return pltpu.make_async_remote_copy(
            src_ref=source,
            dst_ref=target,
            send_sem=send_m.at[slot],
            recv_sem=recv_m.at[slot],
            device_id=partner,
            device_id_type=MESH,
        )

    swap_mine = swap(0, summ.at[1 - core], both.at[core])
    swap_rest = swap(1, summ.at[0], other)
    swap_mine.start()

    @pl.when(core == 0)
    def _():
        swap_rest.start()

    both[core] = summ[core]
    swap_mine.wait_recv()
    for pair in range(chips):
        joined[pair] = advance(both[1, pair], both[0, pair])

    def gather(way):
        return pltpu.make_async_remote_copy(
            src_ref=joined.at[there(way)],
            dst_ref=parts.at[chip],
            send_sem=send_a.at[way],
            recv_sem=recv_a.at[chips - way],
            device_id=device(way),
            device_id_type=MESH,
        )

    for way in ways:
        gather(way).start()
    parts[chip] = joined[chip]

    count = min(2, chips)

    def read(group, _):
        read_step(group, count, own, reach, reads, rights)
        return 0

    lax.fori_loop(0, chips // count, read, 0)

    for way in ways:
        gather(way).wait_recv()

    levels = [[parts[place] for place in range(chips)]]
    while len(levels[-1]) > 1:
        below = levels[-1]
        levels.append([advance(below[i + 1], below[i]) for i in range(0, len(below), 2)])
    totals[chain] = levels[-1][0]

    def pass_on(step):
        return pltpu.make_async_remote_copy(
            src_ref=totals.at[chain],
            dst_ref=totals.at[chain],
            send_sem=send_b.at[step],
            recv_sem=recv_b.at[step],
            device_id={"chain": lax.rem(chain + step, chains)},
            device_id_type=MESH,
        )

    def take(step):
        return pltpu.make_async_remote_copy(
            src_ref=totals.at[chain],
            dst_ref=totals.at[lax.rem(chain - step + chains, chains)],
            send_sem=send_b.at[step],
            recv_sem=recv_b.at[step],
            device_id={"chain": lax.rem(chain + step, chains)},
            device_id_type=MESH,
        )

    for step in range(chains - 1, 0, -1):

        @pl.when(chain + step < chains)
        def _():
            pass_on(step).start()

    row = lax.broadcasted_iota(jnp.int32, (WIDTH, PAIR), 0)
    lane = lax.broadcasted_iota(jnp.int32, (WIDTH, PAIR), 1)
    before = [None]
    for level in reversed(levels[:-1]):
        spread = []
        for i, state in enumerate(before):
            here = level[2 * i]
            spread += [state, here if state is None else advance(here, state)]
        before = spread
    before[0] = jnp.where(lane == row + WIDTH, 1.0, 0.0)
    for place in range(chips):
        starts[place] = before[place]

    for step in range(1, chains):

        @pl.when(chain >= step)
        def _():
            take(step).wait_recv()

    state = jnp.where(chain > 0, totals[0], 0.0)
    for place in range(1, chains - 1):
        state = jnp.where(place < chain, advance(totals[place], state), state)
    state = jnp.where(lane < WIDTH, state, 0.0)

    entry = halves(rows(jnp.zeros((WIDTH, PAIR), F32), state))
    for place in range(chips):
        moved = product(halves(starts[place]), entry) + starts[place]
        outbox[place] = lanes(moved[: WIDTH // 2, :WIDTH], moved[WIDTH // 2 :, :WIDTH])

    def reply(way):
        return pltpu.make_async_remote_copy(
            src_ref=outbox.at[there(way)],
            dst_ref=inbox.at[core, chip],
            send_sem=send_c.at[way],
            recv_sem=recv_c.at[chips - way],
            device_id=device(way),
            device_id_type=MESH,
        )

    def hand_on(way):
        return pltpu.make_async_remote_copy(
            src_ref=inbox.at[core, there(way)],
            dst_ref=inbox.at[core, there(way)],
            send_sem=send_f.at[way],
            recv_sem=recv_f.at[way],
            device_id=partner,
            device_id_type=MESH,
        )

    def handed(way):
        return pltpu.make_async_remote_copy(
            src_ref=inbox.at[core, there(way)],
            dst_ref=inbox.at[1 - core, there(way)],
            send_sem=send_f.at[way],
            recv_sem=recv_f.at[way],
            device_id=partner,
            device_id_type=MESH,
        )

    for way in ways:
        reply(way).start()
    inbox[core, chip] = outbox[chip]
    hand_on(0).start()

    @pl.when(core == 1)
    def _():
        swap_rest.wait_recv()

        def fold(pair, _):
            fold_step(pair, own, reach, maps, sums, other, both.at[0])
            return 0

        lax.fori_loop(0, chips, fold, 0)

    for way in reversed(ways):
        reply(chips - way).wait_recv()
        hand_on(way).start()
    for way in [0] + ways[::-1]:
        handed(way).wait_recv()

    def enter(group, _):
        for i in range(count):
            enter_step(group * count + i, own, reach, maps, sums, inbox, out_ref, state_ref)
        return 0

    lax.fori_loop(0, chips // count, enter, 0)

    swap_mine.wait_send()

    @pl.when(core == 0)
    def _():
        swap_rest.wait_send()

    for way in ways:
        gather(way).wait_send()
        reply(way).wait_send()
    for way in [0] + ways:
        hand_on(way).wait_send()
    for step in range(1, chains):

        @pl.when(chain + step < chains)
        def _():
            pass_on(step).wait_send()


def solution(mesh):
    chains, chips = mesh.shape["chain"], mesh.shape["seq"] // 2

    def body(*args):
        tokens, columns = args[0].shape
        heads = columns // WIDTH
        half = WIDTH // 2
        vmem = pl.BlockSpec(memory_space=pltpu.VMEM)
        each = pltpu.VMEM((chips, WIDTH, PAIR), F32)
        sems = pltpu.SemaphoreType.DMA
        return pl.pallas_call(
            functools.partial(kernel, chains, chips),
            in_specs=[pl.BlockSpec(memory_space=pltpu.HBM)] * 7,
            out_specs=[vmem] * 2,
            out_shape=[
                jax.ShapeDtypeStruct((tokens, columns), F32),
                jax.ShapeDtypeStruct((1, heads, WIDTH, WIDTH), F32),
            ],
            scratch_shapes=[
                pltpu.VMEM((tokens, columns), BF16),
                pltpu.VMEM((tokens, columns), BF16),
                pltpu.VMEM((tokens, columns), BF16),
                pltpu.VMEM((tokens, columns), F32),
                pltpu.VMEM((tokens, columns), BF16),
                pltpu.VMEM((heads, WIDTH), F32),
                pltpu.VMEM((heads, WIDTH), F32),
                sems((7,)),
                pltpu.VMEM((tokens, columns), F32),
                pltpu.VMEM((tokens, columns), F32),
                each,
                each,
                pltpu.VMEM((heads, 2 * tokens, 2 * tokens), BF16),
                pltpu.VMEM((heads, 2 * tokens, 2 * PAIR), BF16),
                pltpu.VMEM((2, chips, WIDTH, PAIR), F32),
                pltpu.VMEM((7, tokens, tokens), BF16),
                pltpu.VMEM((2, chips, WIDTH, PAIR), F32),
                each,
                each,
                each,
                each,
                pltpu.VMEM((chains, WIDTH, PAIR), F32),
                pltpu.VMEM((2, chips, half, PAIR), F32),
                pltpu.VMEM((chips, half, PAIR), F32),
                sems((2,)), sems((2,)), sems((chips,)), sems((chips,)), sems((chains,)),
                sems((chains,)), sems((chips,)), sems((chips,)), sems((chips,)), sems((chips,)),
            ],
            compiler_params=pltpu.CompilerParams(
                collective_id=0, has_side_effects=True, vmem_limit_bytes=VMEM_LIMIT
            ),
            name="mix",
        )(*[pltpu.with_memory_space_constraint(x, pltpu.HBM) for x in args])

    wide = P(("chain", "seq"), "head")
    return jax.shard_map(
        body,
        mesh=mesh,
        in_specs=(wide,) * 5 + (P("head", None),) * 2,
        out_specs=(wide, P(("chain", "seq"), "head", None, None)),
        check_vma=False,
    )
```

```python
import functools

import jax
import jax.numpy as jnp
from jax import lax
from jax.experimental import pallas as pl
from jax.experimental.pallas import tpu as pltpu
from jax.sharding import PartitionSpec as P

MESH = pl.DeviceIdType.MESH
WIDTH = 64
PAIR = 2 * WIDTH
VMEM_LIMIT = 40 * 1024 * 1024
F32 = jnp.float32
BF16 = jnp.bfloat16


def halves(x):
    high = x.astype(BF16)
    return high, (x - high.astype(F32)).astype(BF16)


def thirds(x):
    high = x.astype(BF16)
    rest = x - high.astype(F32)
    mid = rest.astype(BF16)
    return high, mid, (rest - mid.astype(F32)).astype(BF16)


def dot(a, b):
    return jnp.dot(a, b, preferred_element_type=F32)


def dot_nt(a, b):
    return lax.dot_general(a, b, (((1,), (1,)), ((), ())), preferred_element_type=F32)


def lanes(*parts):
    return jnp.concatenate(parts, axis=1)


def rows(*parts):
    return jnp.concatenate(parts, axis=0)


def product(x, y):
    right = lanes(*y)
    both = dot(lanes(*x), rows(right, right))
    return both[:, :PAIR] + both[:, PAIR:]


def below_left(x, y, size, held):
    if size < 16:
        return product(x, y)
    cuts = range(0, x[0].shape[0], 2 * size)
    right = lanes(*y)
    at = held * size
    right = rows(*[right[c + at : c + at + size] for c in cuts for _ in range(2)])
    odd = [rows(*[part[c + size : c + 2 * size] for c in cuts]) for part in x]
    lane = lax.broadcasted_iota(jnp.int32, odd[0].shape, 1)
    here = (lane // size) % 2 == held
    moved = pltpu.roll(odd[1], size if held == 0 else PAIR - size, 1)
    both = dot(jnp.where(here, odd[0], moved), right)
    out = both[:, :PAIR] + both[:, PAIR:]
    blank = jnp.zeros((size, PAIR), F32)
    return rows(*[part for c in cuts for part in (blank, out[c // 2 : c // 2 + size])])


def advance(summary, state):
    pad = jnp.zeros((WIDTH, PAIR), F32)
    lane = lax.broadcasted_iota(jnp.int32, (WIDTH, PAIR), 1)
    moved = product(halves(summary), halves(rows(pad, state)))
    return moved + jnp.where(lane < WIDTH, summary, 0.0)


def side_by_side(ref, head):
    return lanes(ref[pl.ds(head, 1), :], ref[pl.ds(head + 1, 1), :])


def same_head():
    row = lax.broadcasted_iota(jnp.int32, (2 * PAIR, PAIR), 0)
    col = lax.broadcasted_iota(jnp.int32, (2 * PAIR, PAIR), 1)
    return jnp.where((row // WIDTH) % 2 == col // WIDTH, 1.0, 0.0).astype(BF16)


def scores_of(left, right, h):
    keep = (lax.broadcasted_iota(jnp.int32, right[0].shape, 1) < WIDTH) == (h == 0)
    high, low = [jnp.where(keep, part, jnp.zeros((), BF16)) for part in right]
    return dot_nt(lanes(*left), lanes(high, high)) + dot_nt(left[0], low)


def local_step(
    w_ref, k_ref, v_ref, a_ref, factor_ref, w_ready, ready,
    shifts, cums, maps, sums, rights, keys, summ, masks,
):
    tokens = k_ref.shape[0]
    half = tokens // 2
    row = lax.broadcasted_iota(jnp.int32, (tokens, tokens), 0)
    col = lax.broadcasted_iota(jnp.int32, (tokens, tokens), 1)
    strict = row > col
    lane = lax.broadcasted_iota(jnp.int32, (tokens, PAIR), 1)
    first = lane < WIDTH
    signs = jnp.where(
        (row >= col) & (col >= half), 1.0, jnp.where((row < col) & (col < half), -1.0, 0.0)
    ).astype(BF16)
    same = same_head()
    srow = lax.broadcasted_iota(jnp.int32, (WIDTH, PAIR), 0)
    slane = lax.broadcasted_iota(jnp.int32, (WIDTH, PAIR), 1)
    diagonal = srow == slane % WIDTH
    sfirst = slane < WIDTH
    zero = jnp.zeros((), F32)

    pairs = range(maps.shape[0])
    w_ready()
    decays = []
    for p in pairs:
        at = pl.ds(p * PAIR, PAIR)
        log_w = w_ref[:, at]
        cum = sum(dot(signs, part) for part in reversed(thirds(log_w)))
        cums[:, at] = cum
        start = cum[0:1] - log_w[0:1]
        last = cum[tokens - 1 : tokens]
        shifts[p : p + 1, :] = jnp.exp(-start)
        decays.append((jnp.exp(cum - log_w), jnp.exp(-cum), jnp.exp(last), jnp.exp(last - start)))
    ready()
    prepared = []
    for p in pairs:
        at = pl.ds(p * PAIR, PAIR)
        k = k_ref[:, at].astype(F32)
        v = v_ref[:, at]
        a = a_ref[:, at].astype(F32)
        ahead, grow, to_end, whole = decays[p]
        removal = k * side_by_side(factor_ref, 2 * p)
        square = dot(lanes(*halves(removal * removal)), same)
        kappa = removal * lax.rsqrt(square + 1e-06 * WIDTH)
        b = a * kappa
        kappa_mid = kappa * ahead
        k_mid = k * grow
        b_mid = b * grow
        left = halves(kappa_mid)
        right = halves(rows(b_mid, k_mid))
        keys[p] = lanes(*right)
        ends = halves(jnp.transpose(lanes(k_mid * to_end, b_mid * -to_end)))
        swapped = pltpu.roll(kappa_mid * shifts[p : p + 1, :], WIDTH, 1)
        whole = pltpu.roll(jnp.broadcast_to(whole, (WIDTH, PAIR)), WIDTH, 1)
        prepared.append((v, left, right, ends, swapped, whole))

    heads = [(p, h) for p in pairs for h in range(2)]
    scores = [scores_of(prepared[p][1], prepared[p][2], h) for p, h in heads]
    lower = [jnp.where(strict, s[:, :tokens], zero) for s in scores]
    mix_key = [halves(jnp.where(strict, s[:, tokens:], zero)) for s in scores]
    values, wanted = [], []
    for i, (p, h) in enumerate(heads):
        v, swapped = prepared[p][0], prepared[p][4]
        mine = first == (h == 0)
        own_v = jnp.where(mine, v, jnp.zeros((), BF16))
        values.append(own_v)
        pushed = dot(lanes(*mix_key[i]), rows(own_v, own_v))
        wanted.append(pushed + jnp.where(mine, zero, swapped))

    lower = [halves(l) for l in lower]
    eye = jnp.where(row == col, 1.0, 0.0).astype(BF16)
    inverse = [(eye - high * masks[0], -low * masks[0]) for high, low in lower]
    size, level = 2, 1
    while size < tokens:
        mask = masks[level]
        edge = [(high * mask, low * mask) for high, low in lower]
        step = [below_left(e, m, size, 0) for e, m in zip(edge, inverse)]
        step = [below_left(m, halves(s), size, 1) for m, s in zip(inverse, step)]
        step = [halves(s) for s in step]
        inverse = [(m[0] - s[0], m[1] - s[1]) for m, s in zip(inverse, step)]
        size, level = 2 * size, level + 1

    removed = [halves(product(m, halves(w))) for m, w in zip(inverse, wanted)]
    outs = []
    for i, (p, h) in enumerate(heads):
        ends = prepared[p][3]
        cut = slice(h * WIDTH, (h + 1) * WIDTH)
        stack = rows(
            *[lanes(e[cut, :], e[PAIR + h * WIDTH : PAIR + (h + 1) * WIDTH, :]) for e in ends]
        )
        right = rows(lanes(values[i], jnp.zeros_like(values[i])), lanes(*removed[i]))
        rights[i] = right
        both = dot(stack, right)
        both = both[:, :PAIR] + both[:, PAIR:]
        outs.append(both[:WIDTH] + both[WIDTH:])
    for p in pairs:
        fade = jnp.where(diagonal, prepared[p][5], zero)
        one = outs[2 * p] + jnp.where(sfirst, zero, fade)
        two = outs[2 * p + 1] + jnp.where(sfirst, fade, zero)
        summ[0, p] = one
        summ[1, p] = pltpu.roll(two, WIDTH, 1)
        maps[p] = jnp.where(sfirst, two, one)
        sums[p] = jnp.where(sfirst, one, two)


def read_step(group, count, r_ref, k_ref, v_ref, gain_ref, shifts, cums, own, reach, rights, keys):
    tokens = own.shape[0]
    row = lax.broadcasted_iota(jnp.int32, (tokens, 2 * tokens), 0)
    col = lax.broadcasted_iota(jnp.int32, (tokens, 2 * tokens), 1)
    incl = row >= col % tokens
    first = lax.broadcasted_iota(jnp.int32, (tokens, PAIR), 1) < WIDTH
    same = same_head()
    prepared = []
    for p in range(count):
        pair = group * count + p
        at = pl.ds(pl.multiple_of(pair * PAIR, PAIR), PAIR)
        r = r_ref[:, at].astype(F32)
        r_mid = r * jnp.exp(cums[:, at])
        gained = r * side_by_side(gain_ref, 2 * pair) * k_ref[:, at].astype(F32)
        bonus = dot(lanes(*halves(gained)), same)
        key = keys[pair]
        prepared.append(
            (
                at,
                halves(r_mid),
                (key[:, :PAIR], key[:, PAIR:]),
                bonus * v_ref[:, at].astype(F32),
                pltpu.roll(r_mid * shifts[pl.ds(pair, 1), :], WIDTH, 1),
            )
        )
    reads = []
    for at, left, right, _, _ in prepared:
        for h in range(2):
            score = scores_of(left, right, h)
            score = lanes(score[:, tokens:], -score[:, :tokens])
            reads.append(rows(*halves(jnp.where(incl, score, 0.0))))
    outs = []
    for i, read in enumerate(reads):
        both = dot(read, rights[group * 2 * count + i])
        both = both[:, :PAIR] + both[:, PAIR:]
        outs.append(both[:tokens] + both[tokens:])
    for p, (at, _, _, bonus, entry) in enumerate(prepared):
        one, two = outs[2 * p], outs[2 * p + 1]
        own[:, at] = bonus + jnp.where(first, one, two)
        reach[:, at] = entry + jnp.where(first, two, one)


def fold_step(pair, own, reach, maps, sums, first, second):
    tokens = own.shape[0]
    low = lax.broadcasted_iota(jnp.int32, (WIDTH, PAIR), 1) < WIDTH
    at = pl.ds(pl.multiple_of(pair * PAIR, PAIR), PAIR)
    one, two = first[pair], pltpu.roll(second[pair], WIDTH, 1)
    right = rows(
        lanes(jnp.where(low, two, 0.0), jnp.where(low, 0.0, two)),
        lanes(jnp.where(low, 0.0, one), jnp.where(low, one, 0.0)),
    )
    high, rest = halves(right)
    left = halves(rows(reach[:, at], maps[pair]))
    moved = dot(lanes(*left), rows(high, high)) + dot(left[0], rest)
    reach[:, at] = moved[:tokens, :PAIR]
    own[:, at] += moved[:tokens, PAIR:]
    maps[pair] = moved[tokens:, :PAIR]
    sums[pair] += moved[tokens:, PAIR:]


def enter_step(pair, own, reach, maps, sums, inbox, out_ref, state_ref):
    tokens = own.shape[0]
    zero = jnp.zeros((WIDTH, WIDTH), F32)
    at = pl.ds(pl.multiple_of(pair * PAIR, PAIR), PAIR)
    one, two = [
        rows(inbox[h, pair][:, :WIDTH], inbox[h, pair][:, WIDTH:]) for h in range(2)
    ]
    entry = halves(rows(lanes(zero, two), lanes(one, zero)))
    moved = product(halves(rows(reach[:, at], maps[pair])), entry)
    out_ref[:, at] = own[:, at] + moved[:tokens]
    after = sums[pair] + moved[tokens:]
    state_ref[0, 2 * pair] = after[:, :WIDTH]
    state_ref[0, 2 * pair + 1] = after[:, WIDTH:]


def kernel(
    chains, chips, r_in, k_in, v_in, w_in, a_in, factor_in, gain_in, out_ref, state_ref,
    r_ref, k_ref, v_ref, w_ref, a_ref, factor_ref, gain_ref, load, shifts, cums,
    own, reach, maps, sums, rights, keys, summ, masks, both, other, joined, parts, starts, totals,
    inbox, outbox, send_m, recv_m, send_a, recv_a, send_b, recv_b, send_c, recv_c, send_f, recv_f,
):
    sources = (w_in, k_in, factor_in, a_in, v_in, r_in, gain_in)
    targets = (w_ref, k_ref, factor_ref, a_ref, v_ref, r_ref, gain_ref)
    loads = [
        pltpu.make_async_copy(source, target, load.at[i])
        for i, (source, target) in enumerate(zip(sources, targets))
    ]
    for copy in loads:
        copy.start()
    chain = lax.axis_index("chain")
    seq = lax.axis_index("seq")
    core = lax.rem(seq, 2)
    chip = seq // 2
    partner = {"seq": seq + 1 - 2 * core}
    barrier = pltpu.get_barrier_semaphore()
    ways = sorted(range(1, chips), key=lambda way: -min(way, chips - way))

    def there(way):
        return lax.rem(chip + way, chips)

    def device(way):
        return {"seq": 2 * there(way) + core}

    def greet(device_id):
        pl.semaphore_signal(barrier, inc=1, device_id=device_id, device_id_type=MESH)

    totals[...] = jnp.zeros_like(totals)
    greet(partner)
    for way in ways:
        greet(device(way))
    for step in range(1, chains):
        greet({"chain": lax.rem(chain + step, chains)})
    row = lax.broadcasted_iota(jnp.int32, masks.shape[1:], 0)
    col = lax.broadcasted_iota(jnp.int32, masks.shape[1:], 1)
    for level in range(masks.shape[0]):
        size = 1 << level
        inside = (row // (2 * size) == col // (2 * size)) & (row // size > col // size)
        masks[level] = jnp.where(inside, 1.0, 0.0).astype(BF16)

    def ready():
        for copy in loads[1:]:
            copy.wait()

    local_step(
        w_ref, k_ref, v_ref, a_ref, factor_ref, loads[0].wait, ready,
        shifts, cums, maps, sums, rights, keys, summ, masks,
    )
    pl.semaphore_wait(barrier, chips + chains - 1)

    def swap(way):
        return pltpu.make_async_remote_copy(
            src_ref=summ.at[1 - core, there(way)],
            dst_ref=both.at[core, there(way)],
            send_sem=send_m.at[way],
            recv_sem=recv_m.at[way],
            device_id=partner,
            device_id_type=MESH,
        )

    swap_rest = pltpu.make_async_remote_copy(
        src_ref=summ.at[0],
        dst_ref=other,
        send_sem=send_m.at[chips],
        recv_sem=recv_m.at[chips],
        device_id=partner,
        device_id_type=MESH,
    )
    order = ways + [0]
    for way in order:
        swap(way).start()

    @pl.when(core == 0)
    def _():
        swap_rest.start()

    both[core] = summ[core]

    def gather(way):
        return pltpu.make_async_remote_copy(
            src_ref=joined.at[there(way)],
            dst_ref=parts.at[chip],
            send_sem=send_a.at[way],
            recv_sem=recv_a.at[chips - way],
            device_id=device(way),
            device_id_type=MESH,
        )

    for at in range(0, chips, 2):
        for way in order[at : at + 2]:
            swap(way).wait_recv()
        made = [advance(both[1, there(way)], both[0, there(way)]) for way in order[at : at + 2]]
        for way, summary in zip(order[at : at + 2], made):
            joined[there(way)] = summary
        for way in order[at : at + 2]:
            if way:
                gather(way).start()
    parts[chip] = joined[chip]

    count = min(2, chips)

    def read(group, _):
        read_step(
            group, count, r_ref, k_ref, v_ref, gain_ref, shifts, cums, own, reach, rights, keys
        )
        return 0

    lax.fori_loop(0, chips // count, read, 0)

    for way in ways:
        gather(way).wait_recv()

    levels = [[parts[place] for place in range(chips)]]
    while len(levels[-1]) > 1:
        below = levels[-1]
        levels.append([advance(below[i + 1], below[i]) for i in range(0, len(below), 2)])
    totals[chain] = levels[-1][0]

    def pass_on(step):
        return pltpu.make_async_remote_copy(
            src_ref=totals.at[chain],
            dst_ref=totals.at[chain],
            send_sem=send_b.at[step],
            recv_sem=recv_b.at[step],
            device_id={"chain": lax.rem(chain + step, chains)},
            device_id_type=MESH,
        )

    def take(step):
        return pltpu.make_async_remote_copy(
            src_ref=totals.at[chain],
            dst_ref=totals.at[lax.rem(chain - step + chains, chains)],
            send_sem=send_b.at[step],
            recv_sem=recv_b.at[step],
            device_id={"chain": lax.rem(chain + step, chains)},
            device_id_type=MESH,
        )

    for step in range(chains - 1, 0, -1):

        @pl.when(chain + step < chains)
        def _():
            pass_on(step).start()

    row = lax.broadcasted_iota(jnp.int32, (WIDTH, PAIR), 0)
    lane = lax.broadcasted_iota(jnp.int32, (WIDTH, PAIR), 1)
    before = [None]
    for level in reversed(levels[:-1]):
        spread = []
        for i, state in enumerate(before):
            here = level[2 * i]
            spread += [state, here if state is None else advance(here, state)]
        before = spread
    before[0] = jnp.where(lane == row + WIDTH, 1.0, 0.0)
    for place in range(chips):
        starts[place] = before[place]

    for step in range(1, chains):

        @pl.when(chain >= step)
        def _():
            take(step).wait_recv()

    state = jnp.where(chain > 0, totals[0], 0.0)
    for place in range(1, chains - 1):
        state = jnp.where(place < chain, advance(totals[place], state), state)
    state = jnp.where(lane < WIDTH, state, 0.0)

    entry = halves(rows(jnp.zeros((WIDTH, PAIR), F32), state))
    for place in range(chips):
        moved = product(halves(starts[place]), entry) + starts[place]
        outbox[place] = lanes(moved[: WIDTH // 2, :WIDTH], moved[WIDTH // 2 :, :WIDTH])

    def reply(way):
        return pltpu.make_async_remote_copy(
            src_ref=outbox.at[there(way)],
            dst_ref=inbox.at[core, chip],
            send_sem=send_c.at[way],
            recv_sem=recv_c.at[chips - way],
            device_id=device(way),
            device_id_type=MESH,
        )

    def hand_on(way):
        return pltpu.make_async_remote_copy(
            src_ref=inbox.at[core, there(way)],
            dst_ref=inbox.at[core, there(way)],
            send_sem=send_f.at[way],
            recv_sem=recv_f.at[way],
            device_id=partner,
            device_id_type=MESH,
        )

    def handed(way):
        return pltpu.make_async_remote_copy(
            src_ref=inbox.at[core, there(way)],
            dst_ref=inbox.at[1 - core, there(way)],
            send_sem=send_f.at[way],
            recv_sem=recv_f.at[way],
            device_id=partner,
            device_id_type=MESH,
        )

    for way in ways:
        reply(way).start()
    inbox[core, chip] = outbox[chip]
    hand_on(0).start()

    @pl.when(core == 1)
    def _():
        swap_rest.wait_recv()

        def fold(pair, _):
            fold_step(pair, own, reach, maps, sums, other, both.at[0])
            return 0

        lax.fori_loop(0, chips, fold, 0)

    turn = [0] + ways[::-1]
    for way in turn[1:]:
        reply(chips - way).wait_recv()
        hand_on(way).start()
    for at in range(0, chips, 4):
        for way in turn[at : at + 4]:
            handed(way).wait_recv()
        for way in turn[at : at + 4]:
            enter_step(there(way), own, reach, maps, sums, inbox, out_ref, state_ref)

    for way in order:
        swap(way).wait_send()

    @pl.when(core == 0)
    def _():
        swap_rest.wait_send()

    for way in ways:
        gather(way).wait_send()
        reply(way).wait_send()
    for way in [0] + ways:
        hand_on(way).wait_send()
    for step in range(1, chains):

        @pl.when(chain + step < chains)
        def _():
            pass_on(step).wait_send()


def deliver_kernel(out_ref, state_ref, out_hbm, state_hbm, sems):
    copies = [
        pltpu.make_async_copy(out_ref, out_hbm, sems.at[0]),
        pltpu.make_async_copy(state_ref, state_hbm, sems.at[1]),
    ]
    for copy in copies:
        copy.start()
    for copy in copies:
        copy.wait()


def deliver(*results):
    return pl.pallas_call(
        deliver_kernel,
        in_specs=[pl.BlockSpec(memory_space=pltpu.VMEM)] * 2,
        out_specs=[pl.BlockSpec(memory_space=pltpu.HBM)] * 2,
        out_shape=[jax.ShapeDtypeStruct(x.shape, x.dtype) for x in results],
        scratch_shapes=[pltpu.SemaphoreType.DMA((2,))],
        compiler_params=pltpu.CompilerParams(vmem_limit_bytes=VMEM_LIMIT),
        name="deliver",
    )(*results)


def solution(mesh):
    chains, chips = mesh.shape["chain"], mesh.shape["seq"] // 2

    def body(*args):
        tokens, columns = args[0].shape
        heads = columns // WIDTH
        half = WIDTH // 2
        vmem = pl.BlockSpec(memory_space=pltpu.VMEM)
        each = pltpu.VMEM((chips, WIDTH, PAIR), F32)
        sems = pltpu.SemaphoreType.DMA
        results = pl.pallas_call(
            functools.partial(kernel, chains, chips),
            in_specs=[pl.BlockSpec(memory_space=pltpu.HBM)] * 7,
            out_specs=[vmem] * 2,
            out_shape=[
                jax.ShapeDtypeStruct((tokens, columns), F32),
                jax.ShapeDtypeStruct((1, heads, WIDTH, WIDTH), F32),
            ],
            scratch_shapes=[
                pltpu.VMEM((tokens, columns), BF16),
                pltpu.VMEM((tokens, columns), BF16),
                pltpu.VMEM((tokens, columns), BF16),
                pltpu.VMEM((tokens, columns), F32),
                pltpu.VMEM((tokens, columns), BF16),
                pltpu.VMEM((heads, WIDTH), F32),
                pltpu.VMEM((heads, WIDTH), F32),
                sems((7,)),
                pltpu.VMEM((chips, PAIR), F32),
                pltpu.VMEM((tokens, columns), F32),
                pltpu.VMEM((tokens, columns), F32),
                pltpu.VMEM((tokens, columns), F32),
                each,
                each,
                pltpu.VMEM((heads, 2 * tokens, 2 * PAIR), BF16),
                pltpu.VMEM((chips, 2 * tokens, 2 * PAIR), BF16),
                pltpu.VMEM((2, chips, WIDTH, PAIR), F32),
                pltpu.VMEM((7, tokens, tokens), BF16),
                pltpu.VMEM((2, chips, WIDTH, PAIR), F32),
                each,
                each,
                each,
                each,
                pltpu.VMEM((chains, WIDTH, PAIR), F32),
                pltpu.VMEM((2, chips, half, PAIR), F32),
                pltpu.VMEM((chips, half, PAIR), F32),
                sems((chips + 1,)), sems((chips + 1,)), sems((chips,)), sems((chips,)),
                sems((chains,)), sems((chains,)), sems((chips,)), sems((chips,)), sems((chips,)), sems((chips,)),
            ],
            compiler_params=pltpu.CompilerParams(
                collective_id=0, has_side_effects=True, vmem_limit_bytes=VMEM_LIMIT
            ),
            name="mix",
        )(*[pltpu.with_memory_space_constraint(x, pltpu.HBM) for x in args])
        return deliver(*results)

    wide = P(("chain", "seq"), "head")
    return jax.shard_map(
        body,
        mesh=mesh,
        in_specs=(wide,) * 5 + (P("head", None),) * 2,
        out_specs=(wide, P(("chain", "seq"), "head", None, None)),
        check_vma=False,
    )
```

```python
import functools

import jax
import jax.numpy as jnp
from jax import lax
from jax.experimental import pallas as pl
from jax.experimental.pallas import tpu as pltpu
from jax.sharding import PartitionSpec as P

MESH = pl.DeviceIdType.MESH
WIDTH = 64
PAIR = 2 * WIDTH
VMEM_LIMIT = 40 * 1024 * 1024
F32 = jnp.float32
BF16 = jnp.bfloat16


def halves(x):
    high = x.astype(BF16)
    return high, (x - high.astype(F32)).astype(BF16)


def thirds(x):
    high = x.astype(BF16)
    rest = x - high.astype(F32)
    mid = rest.astype(BF16)
    return high, mid, (rest - mid.astype(F32)).astype(BF16)


def dot(a, b):
    return jnp.dot(a, b, preferred_element_type=F32)


def dot_nt(a, b):
    return lax.dot_general(a, b, (((1,), (1,)), ((), ())), preferred_element_type=F32)


def lanes(*parts):
    return jnp.concatenate(parts, axis=1)


def rows(*parts):
    return jnp.concatenate(parts, axis=0)


def product(x, y):
    right = lanes(*y)
    both = dot(lanes(*x), rows(right, right))
    return both[:, :PAIR] + both[:, PAIR:]


def below_left(x, y, size, held):
    if size < 16:
        return product(x, y)
    cuts = range(0, x[0].shape[0], 2 * size)
    right = lanes(*y)
    at = held * size
    right = rows(*[right[c + at : c + at + size] for c in cuts for _ in range(2)])
    odd = [rows(*[part[c + size : c + 2 * size] for c in cuts]) for part in x]
    lane = lax.broadcasted_iota(jnp.int32, odd[0].shape, 1)
    here = (lane // size) % 2 == held
    moved = pltpu.roll(odd[1], size if held == 0 else PAIR - size, 1)
    both = dot(jnp.where(here, odd[0], moved), right)
    out = both[:, :PAIR] + both[:, PAIR:]
    blank = jnp.zeros((size, PAIR), F32)
    return rows(*[part for c in cuts for part in (blank, out[c // 2 : c // 2 + size])])


def advance(summary, state):
    pad = jnp.zeros((WIDTH, PAIR), F32)
    lane = lax.broadcasted_iota(jnp.int32, (WIDTH, PAIR), 1)
    moved = product(halves(summary), halves(rows(pad, state)))
    return moved + jnp.where(lane < WIDTH, summary, 0.0)


def side_by_side(ref, head):
    return lanes(ref[pl.ds(head, 1), :], ref[pl.ds(head + 1, 1), :])


def same_head():
    row = lax.broadcasted_iota(jnp.int32, (2 * PAIR, PAIR), 0)
    col = lax.broadcasted_iota(jnp.int32, (2 * PAIR, PAIR), 1)
    return jnp.where((row // WIDTH) % 2 == col // WIDTH, 1.0, 0.0).astype(BF16)


def scores_of(left, right, h):
    keep = (lax.broadcasted_iota(jnp.int32, right[0].shape, 1) < WIDTH) == (h == 0)
    high, low = [jnp.where(keep, part, jnp.zeros((), BF16)) for part in right]
    return dot_nt(lanes(*left), lanes(high, high)) + dot_nt(left[0], low)


def local_step(
    places, w_ref, k_ref, v_ref, a_ref, factor_ref, w_ready, ready,
    shifts, cums, maps, sums, rights, keys, summ, masks,
):
    tokens = k_ref.shape[0]
    half = tokens // 2
    row = lax.broadcasted_iota(jnp.int32, (tokens, tokens), 0)
    col = lax.broadcasted_iota(jnp.int32, (tokens, tokens), 1)
    strict = row > col
    lane = lax.broadcasted_iota(jnp.int32, (tokens, PAIR), 1)
    first = lane < WIDTH
    signs = jnp.where(
        (row >= col) & (col >= half), 1.0, jnp.where((row < col) & (col < half), -1.0, 0.0)
    ).astype(BF16)
    same = same_head()
    srow = lax.broadcasted_iota(jnp.int32, (WIDTH, PAIR), 0)
    slane = lax.broadcasted_iota(jnp.int32, (WIDTH, PAIR), 1)
    diagonal = srow == slane % WIDTH
    sfirst = slane < WIDTH
    zero = jnp.zeros((), F32)

    pairs = range(len(places))
    spans = [pl.ds(pl.multiple_of(place * PAIR, PAIR), PAIR) for place in places]
    w_ready()
    decays = []
    for p in pairs:
        at = spans[p]
        log_w = w_ref[:, at]
        cum = sum(dot(signs, part) for part in reversed(thirds(log_w)))
        cums[:, at] = cum
        start = cum[0:1] - log_w[0:1]
        last = cum[tokens - 1 : tokens]
        shift = jnp.exp(-start)
        shifts[pl.ds(places[p], 1), :] = shift
        decays.append(
            (jnp.exp(cum - log_w), jnp.exp(-cum), jnp.exp(last), jnp.exp(last - start), shift)
        )
    ready()
    prepared = []
    for p in pairs:
        at = spans[p]
        k = k_ref[:, at].astype(F32)
        v = v_ref[:, at]
        a = a_ref[:, at].astype(F32)
        ahead, grow, to_end, whole, shift = decays[p]
        removal = k * side_by_side(factor_ref, 2 * places[p])
        square = dot(lanes(*halves(removal * removal)), same)
        kappa = removal * lax.rsqrt(square + 1e-06 * WIDTH)
        b = a * kappa
        kappa_mid = kappa * ahead
        k_mid = k * grow
        b_mid = b * grow
        left = halves(kappa_mid)
        right = halves(rows(b_mid, k_mid))
        keys[places[p]] = lanes(*right)
        ends = halves(jnp.transpose(lanes(k_mid * to_end, b_mid * -to_end)))
        swapped = pltpu.roll(kappa_mid * shift, WIDTH, 1)
        whole = pltpu.roll(jnp.broadcast_to(whole, (WIDTH, PAIR)), WIDTH, 1)
        prepared.append((v, left, right, ends, swapped, whole))

    heads = [(p, h) for p in pairs for h in range(2)]
    scores = [scores_of(prepared[p][1], prepared[p][2], h) for p, h in heads]
    lower = [jnp.where(strict, s[:, :tokens], zero) for s in scores]
    mix_key = [halves(jnp.where(strict, s[:, tokens:], zero)) for s in scores]
    values, wanted = [], []
    for i, (p, h) in enumerate(heads):
        v, swapped = prepared[p][0], prepared[p][4]
        mine = first == (h == 0)
        own_v = jnp.where(mine, v, jnp.zeros((), BF16))
        values.append(own_v)
        pushed = dot(lanes(*mix_key[i]), rows(own_v, own_v))
        wanted.append(pushed + jnp.where(mine, zero, swapped))

    yield

    lower = [halves(l) for l in lower]
    eye = jnp.where(row == col, 1.0, 0.0).astype(BF16)
    inverse = [(eye - high * masks[0], -low * masks[0]) for high, low in lower]
    size, level = 2, 1
    while size < tokens:
        mask = masks[level]
        edge = [(high * mask, low * mask) for high, low in lower]
        step = [below_left(e, m, size, 0) for e, m in zip(edge, inverse)]
        step = [below_left(m, halves(s), size, 1) for m, s in zip(inverse, step)]
        step = [halves(s) for s in step]
        inverse = [(m[0] - s[0], m[1] - s[1]) for m, s in zip(inverse, step)]
        size, level = 2 * size, level + 1

    removed = [halves(product(m, halves(w))) for m, w in zip(inverse, wanted)]
    outs = []
    for i, (p, h) in enumerate(heads):
        ends = prepared[p][3]
        cut = slice(h * WIDTH, (h + 1) * WIDTH)
        stack = rows(
            *[lanes(e[cut, :], e[PAIR + h * WIDTH : PAIR + (h + 1) * WIDTH, :]) for e in ends]
        )
        right = rows(lanes(values[i], jnp.zeros_like(values[i])), lanes(*removed[i]))
        rights[2 * places[p] + h] = right
        both = dot(stack, right)
        both = both[:, :PAIR] + both[:, PAIR:]
        outs.append(both[:WIDTH] + both[WIDTH:])
    for p in pairs:
        fade = jnp.where(diagonal, prepared[p][5], zero)
        one = outs[2 * p] + jnp.where(sfirst, zero, fade)
        two = outs[2 * p + 1] + jnp.where(sfirst, fade, zero)
        summ[0, places[p]] = one
        summ[1, places[p]] = pltpu.roll(two, WIDTH, 1)
        maps[places[p]] = jnp.where(sfirst, two, one)
        sums[places[p]] = jnp.where(sfirst, one, two)


def read_step(group, count, r_ref, k_ref, v_ref, gain_ref, shifts, cums, own, reach, rights, keys):
    tokens = own.shape[0]
    row = lax.broadcasted_iota(jnp.int32, (tokens, 2 * tokens), 0)
    col = lax.broadcasted_iota(jnp.int32, (tokens, 2 * tokens), 1)
    incl = row >= col % tokens
    first = lax.broadcasted_iota(jnp.int32, (tokens, PAIR), 1) < WIDTH
    same = same_head()
    prepared = []
    for p in range(count):
        pair = group * count + p
        at = pl.ds(pl.multiple_of(pair * PAIR, PAIR), PAIR)
        r = r_ref[:, at].astype(F32)
        r_mid = r * jnp.exp(cums[:, at])
        gained = r * side_by_side(gain_ref, 2 * pair) * k_ref[:, at].astype(F32)
        bonus = dot(lanes(*halves(gained)), same)
        key = keys[pair]
        prepared.append(
            (
                at,
                halves(r_mid),
                (key[:, :PAIR], key[:, PAIR:]),
                bonus * v_ref[:, at].astype(F32),
                pltpu.roll(r_mid * shifts[pl.ds(pair, 1), :], WIDTH, 1),
            )
        )
    reads = []
    for at, left, right, _, _ in prepared:
        for h in range(2):
            score = scores_of(left, right, h)
            score = lanes(score[:, tokens:], -score[:, :tokens])
            reads.append(rows(*halves(jnp.where(incl, score, 0.0))))
    outs = []
    for i, read in enumerate(reads):
        both = dot(read, rights[group * 2 * count + i])
        both = both[:, :PAIR] + both[:, PAIR:]
        outs.append(both[:tokens] + both[tokens:])
    for p, (at, _, _, bonus, entry) in enumerate(prepared):
        one, two = outs[2 * p], outs[2 * p + 1]
        own[:, at] = bonus + jnp.where(first, one, two)
        reach[:, at] = entry + jnp.where(first, two, one)


def fold_step(pair, own, reach, maps, sums, first, second):
    tokens = own.shape[0]
    low = lax.broadcasted_iota(jnp.int32, (WIDTH, PAIR), 1) < WIDTH
    at = pl.ds(pl.multiple_of(pair * PAIR, PAIR), PAIR)
    one, two = first[pair], pltpu.roll(second[pair], WIDTH, 1)
    right = rows(
        lanes(jnp.where(low, two, 0.0), jnp.where(low, 0.0, two)),
        lanes(jnp.where(low, 0.0, one), jnp.where(low, one, 0.0)),
    )
    high, rest = halves(right)
    left = halves(rows(reach[:, at], maps[pair]))
    moved = dot(lanes(*left), rows(high, high)) + dot(left[0], rest)
    reach[:, at] = moved[:tokens, :PAIR]
    own[:, at] += moved[:tokens, PAIR:]
    maps[pair] = moved[tokens:, :PAIR]
    sums[pair] += moved[tokens:, PAIR:]


def enter_step(pair, own, reach, maps, sums, inbox, out_ref, state_ref):
    tokens = own.shape[0]
    zero = jnp.zeros((WIDTH, WIDTH), F32)
    at = pl.ds(pl.multiple_of(pair * PAIR, PAIR), PAIR)
    one, two = [
        rows(inbox[h, pair][:, :WIDTH], inbox[h, pair][:, WIDTH:]) for h in range(2)
    ]
    entry = halves(rows(lanes(zero, two), lanes(one, zero)))
    moved = product(halves(rows(reach[:, at], maps[pair])), entry)
    out_ref[:, at] = own[:, at] + moved[:tokens]
    after = sums[pair] + moved[tokens:]
    state_ref[0, 2 * pair] = after[:, :WIDTH]
    state_ref[0, 2 * pair + 1] = after[:, WIDTH:]


def kernel(
    chains, chips, r_in, k_in, v_in, w_in, a_in, factor_in, gain_in, out_ref, state_ref,
    r_ref, k_ref, v_ref, w_ref, a_ref, factor_ref, gain_ref, load, shifts, cums,
    own, reach, maps, sums, rights, keys, summ, masks, both, other, joined, parts, starts, totals,
    inbox, outbox, send_m, recv_m, send_a, recv_a, send_b, recv_b, send_c, recv_c, send_f, recv_f,
):
    sources = (w_in, k_in, factor_in, a_in, v_in, r_in, gain_in)
    targets = (w_ref, k_ref, factor_ref, a_ref, v_ref, r_ref, gain_ref)
    loads = [
        pltpu.make_async_copy(source, target, load.at[i])
        for i, (source, target) in enumerate(zip(sources, targets))
    ]
    for copy in loads:
        copy.start()
    chain = lax.axis_index("chain")
    seq = lax.axis_index("seq")
    core = lax.rem(seq, 2)
    chip = seq // 2
    partner = {"seq": seq + 1 - 2 * core}
    barrier = pltpu.get_barrier_semaphore()
    ways = sorted(range(1, chips), key=lambda way: -min(way, chips - way))

    def there(way):
        return lax.rem(chip + way, chips)

    def device(way):
        return {"seq": 2 * there(way) + core}

    def greet(device_id):
        pl.semaphore_signal(barrier, inc=1, device_id=device_id, device_id_type=MESH)

    totals[...] = jnp.zeros_like(totals)
    greet(partner)
    for way in ways:
        greet(device(way))
    for step in range(1, chains):
        greet({"chain": lax.rem(chain + step, chains)})
    row = lax.broadcasted_iota(jnp.int32, masks.shape[1:], 0)
    col = lax.broadcasted_iota(jnp.int32, masks.shape[1:], 1)
    for level in range(masks.shape[0]):
        size = 1 << level
        inside = (row // (2 * size) == col // (2 * size)) & (row // size > col // size)
        masks[level] = jnp.where(inside, 1.0, 0.0).astype(BF16)

    def ready():
        for copy in loads[1:]:
            copy.wait()

    order = ways + [0]
    half = chips // 2

    def local(ways_of, w_ready, ready):
        return local_step(
            [there(way) for way in ways_of], w_ref, k_ref, v_ref, a_ref, factor_ref,
            w_ready, ready, shifts, cums, maps, sums, rights, keys, summ, masks,
        )

    def swap(way):
        return pltpu.make_async_remote_copy(
            src_ref=summ.at[1 - core, there(way)],
            dst_ref=both.at[core, there(way)],
            send_sem=send_m.at[way],
            recv_sem=recv_m.at[way],
            device_id=partner,
            device_id_type=MESH,
        )

    swap_rest = pltpu.make_async_remote_copy(
        src_ref=summ.at[0],
        dst_ref=other,
        send_sem=send_m.at[chips],
        recv_sem=recv_m.at[chips],
        device_id=partner,
        device_id_type=MESH,
    )
    def gather(way):
        return pltpu.make_async_remote_copy(
            src_ref=joined.at[there(way)],
            dst_ref=parts.at[chip],
            send_sem=send_a.at[way],
            recv_sem=recv_a.at[chips - way],
            device_id=device(way),
            device_id_type=MESH,
        )

    def offer(ways_of):
        for way in ways_of:
            swap(way).start()
        for way in ways_of:
            both[core, there(way)] = summ[core, there(way)]

    def join(ways_of):
        for way in ways_of:
            swap(way).wait_recv()
        made = [advance(both[1, there(way)], both[0, there(way)]) for way in ways_of]
        for way, summary in zip(ways_of, made):
            joined[there(way)] = summary
        for way in ways_of:
            if way:
                gather(way).start()

    for _ in local(order[:half], loads[0].wait, ready):
        pass
    pl.semaphore_wait(barrier, chips + chains - 1)
    offer(order[:half])
    rest = local(order[half:], lambda: None, lambda: None)
    next(rest)
    join(order[:half])
    for _ in rest:
        pass
    offer(order[half:])

    @pl.when(core == 0)
    def _():
        swap_rest.start()

    for at in range(half, chips, 2):
        join(order[at : min(at + 2, chips)])
    parts[chip] = joined[chip]

    count = min(2, chips)

    def read(group, _):
        read_step(
            group, count, r_ref, k_ref, v_ref, gain_ref, shifts, cums, own, reach, rights, keys
        )
        return 0

    lax.fori_loop(0, chips // count, read, 0)

    for way in ways:
        gather(way).wait_recv()

    levels = [[parts[place] for place in range(chips)]]
    while len(levels[-1]) > 1:
        below = levels[-1]
        levels.append([advance(below[i + 1], below[i]) for i in range(0, len(below), 2)])
    totals[chain] = levels[-1][0]

    def pass_on(step):
        return pltpu.make_async_remote_copy(
            src_ref=totals.at[chain],
            dst_ref=totals.at[chain],
            send_sem=send_b.at[step],
            recv_sem=recv_b.at[step],
            device_id={"chain": lax.rem(chain + step, chains)},
            device_id_type=MESH,
        )

    def take(step):
        return pltpu.make_async_remote_copy(
            src_ref=totals.at[chain],
            dst_ref=totals.at[lax.rem(chain - step + chains, chains)],
            send_sem=send_b.at[step],
            recv_sem=recv_b.at[step],
            device_id={"chain": lax.rem(chain + step, chains)},
            device_id_type=MESH,
        )

    for step in range(chains - 1, 0, -1):

        @pl.when(chain + step < chains)
        def _():
            pass_on(step).start()

    row = lax.broadcasted_iota(jnp.int32, (WIDTH, PAIR), 0)
    lane = lax.broadcasted_iota(jnp.int32, (WIDTH, PAIR), 1)
    before = [None]
    for level in reversed(levels[:-1]):
        spread = []
        for i, state in enumerate(before):
            here = level[2 * i]
            spread += [state, here if state is None else advance(here, state)]
        before = spread
    before[0] = jnp.where(lane == row + WIDTH, 1.0, 0.0)
    for place in range(chips):
        starts[place] = before[place]

    for step in range(1, chains):

        @pl.when(chain >= step)
        def _():
            take(step).wait_recv()

    state = jnp.where(chain > 0, totals[0], 0.0)
    for place in range(1, chains - 1):
        state = jnp.where(place < chain, advance(totals[place], state), state)
    state = jnp.where(lane < WIDTH, state, 0.0)

    entry = halves(rows(jnp.zeros((WIDTH, PAIR), F32), state))
    for place in range(chips):
        moved = product(halves(starts[place]), entry) + starts[place]
        outbox[place] = lanes(moved[: WIDTH // 2, :WIDTH], moved[WIDTH // 2 :, :WIDTH])

    def reply(way):
        return pltpu.make_async_remote_copy(
            src_ref=outbox.at[there(way)],
            dst_ref=inbox.at[core, chip],
            send_sem=send_c.at[way],
            recv_sem=recv_c.at[chips - way],
            device_id=device(way),
            device_id_type=MESH,
        )

    def hand_on(way):
        return pltpu.make_async_remote_copy(
            src_ref=inbox.at[core, there(way)],
            dst_ref=inbox.at[core, there(way)],
            send_sem=send_f.at[way],
            recv_sem=recv_f.at[way],
            device_id=partner,
            device_id_type=MESH,
        )

    def handed(way):
        return pltpu.make_async_remote_copy(
            src_ref=inbox.at[core, there(way)],
            dst_ref=inbox.at[1 - core, there(way)],
            send_sem=send_f.at[way],
            recv_sem=recv_f.at[way],
            device_id=partner,
            device_id_type=MESH,
        )

    for way in ways:
        reply(way).start()
    inbox[core, chip] = outbox[chip]
    hand_on(0).start()

    @pl.when(core == 1)
    def _():
        swap_rest.wait_recv()

        def fold(pair, _):
            fold_step(pair, own, reach, maps, sums, other, both.at[0])
            return 0

        lax.fori_loop(0, chips, fold, 0)

    turn = [0] + ways[::-1]
    for way in turn[1:]:
        reply(chips - way).wait_recv()
        hand_on(way).start()
    for at in range(0, chips, 4):
        for way in turn[at : at + 4]:
            handed(way).wait_recv()
        for way in turn[at : at + 4]:
            enter_step(there(way), own, reach, maps, sums, inbox, out_ref, state_ref)

    for way in order:
        swap(way).wait_send()

    @pl.when(core == 0)
    def _():
        swap_rest.wait_send()

    for way in ways:
        gather(way).wait_send()
        reply(way).wait_send()
    for way in [0] + ways:
        hand_on(way).wait_send()
    for step in range(1, chains):

        @pl.when(chain + step < chains)
        def _():
            pass_on(step).wait_send()


def deliver_kernel(out_ref, state_ref, out_hbm, state_hbm, sems):
    copies = [
        pltpu.make_async_copy(out_ref, out_hbm, sems.at[0]),
        pltpu.make_async_copy(state_ref, state_hbm, sems.at[1]),
    ]
    for copy in copies:
        copy.start()
    for copy in copies:
        copy.wait()


def deliver(*results):
    return pl.pallas_call(
        deliver_kernel,
        in_specs=[pl.BlockSpec(memory_space=pltpu.VMEM)] * 2,
        out_specs=[pl.BlockSpec(memory_space=pltpu.HBM)] * 2,
        out_shape=[jax.ShapeDtypeStruct(x.shape, x.dtype) for x in results],
        scratch_shapes=[pltpu.SemaphoreType.DMA((2,))],
        compiler_params=pltpu.CompilerParams(vmem_limit_bytes=VMEM_LIMIT),
        name="deliver",
    )(*results)


def solution(mesh):
    chains, chips = mesh.shape["chain"], mesh.shape["seq"] // 2

    def body(*args):
        tokens, columns = args[0].shape
        heads = columns // WIDTH
        half = WIDTH // 2
        vmem = pl.BlockSpec(memory_space=pltpu.VMEM)
        each = pltpu.VMEM((chips, WIDTH, PAIR), F32)
        sems = pltpu.SemaphoreType.DMA
        results = pl.pallas_call(
            functools.partial(kernel, chains, chips),
            in_specs=[pl.BlockSpec(memory_space=pltpu.HBM)] * 7,
            out_specs=[vmem] * 2,
            out_shape=[
                jax.ShapeDtypeStruct((tokens, columns), F32),
                jax.ShapeDtypeStruct((1, heads, WIDTH, WIDTH), F32),
            ],
            scratch_shapes=[
                pltpu.VMEM((tokens, columns), BF16),
                pltpu.VMEM((tokens, columns), BF16),
                pltpu.VMEM((tokens, columns), BF16),
                pltpu.VMEM((tokens, columns), F32),
                pltpu.VMEM((tokens, columns), BF16),
                pltpu.VMEM((heads, WIDTH), F32),
                pltpu.VMEM((heads, WIDTH), F32),
                sems((7,)),
                pltpu.VMEM((chips, PAIR), F32),
                pltpu.VMEM((tokens, columns), F32),
                pltpu.VMEM((tokens, columns), F32),
                pltpu.VMEM((tokens, columns), F32),
                each,
                each,
                pltpu.VMEM((heads, 2 * tokens, 2 * PAIR), BF16),
                pltpu.VMEM((chips, 2 * tokens, 2 * PAIR), BF16),
                pltpu.VMEM((2, chips, WIDTH, PAIR), F32),
                pltpu.VMEM((7, tokens, tokens), BF16),
                pltpu.VMEM((2, chips, WIDTH, PAIR), F32),
                each,
                each,
                each,
                each,
                pltpu.VMEM((chains, WIDTH, PAIR), F32),
                pltpu.VMEM((2, chips, half, PAIR), F32),
                pltpu.VMEM((chips, half, PAIR), F32),
                sems((chips + 1,)), sems((chips + 1,)), sems((chips,)), sems((chips,)),
                sems((chains,)), sems((chains,)), sems((chips,)), sems((chips,)), sems((chips,)), sems((chips,)),
            ],
            compiler_params=pltpu.CompilerParams(
                collective_id=0, has_side_effects=True, vmem_limit_bytes=VMEM_LIMIT
            ),
            name="mix",
        )(*[pltpu.with_memory_space_constraint(x, pltpu.HBM) for x in args])
        return deliver(*results)

    wide = P(("chain", "seq"), "head")
    return jax.shard_map(
        body,
        mesh=mesh,
        in_specs=(wide,) * 5 + (P("head", None),) * 2,
        out_specs=(wide, P(("chain", "seq"), "head", None, None)),
        check_vma=False,
    )
```

```python
import functools

import jax
import jax.numpy as jnp
from jax import lax
from jax.experimental import pallas as pl
from jax.experimental.pallas import tpu as pltpu
from jax.sharding import PartitionSpec as P

MESH = pl.DeviceIdType.MESH
WIDTH = 64
PAIR = 2 * WIDTH
VMEM_LIMIT = 40 * 1024 * 1024
F32 = jnp.float32
BF16 = jnp.bfloat16


def halves(x):
    high = x.astype(BF16)
    return high, (x - high.astype(F32)).astype(BF16)


def thirds(x):
    high = x.astype(BF16)
    rest = x - high.astype(F32)
    mid = rest.astype(BF16)
    return high, mid, (rest - mid.astype(F32)).astype(BF16)


def dot(a, b):
    return jnp.dot(a, b, preferred_element_type=F32)


def dot_nt(a, b):
    return lax.dot_general(a, b, (((1,), (1,)), ((), ())), preferred_element_type=F32)


def lanes(*parts):
    return jnp.concatenate(parts, axis=1)


def rows(*parts):
    return jnp.concatenate(parts, axis=0)


def product(x, y):
    right = lanes(*y)
    both = dot(lanes(*x), rows(right, right))
    return both[:, :PAIR] + both[:, PAIR:]


def below_left(x, y, size, held):
    if size < 16:
        return product(x, y)
    cuts = range(0, x[0].shape[0], 2 * size)
    right = lanes(*y)
    at = held * size
    right = rows(*[right[c + at : c + at + size] for c in cuts for _ in range(2)])
    odd = [rows(*[part[c + size : c + 2 * size] for c in cuts]) for part in x]
    lane = lax.broadcasted_iota(jnp.int32, odd[0].shape, 1)
    here = (lane // size) % 2 == held
    moved = pltpu.roll(odd[1], size if held == 0 else PAIR - size, 1)
    both = dot(jnp.where(here, odd[0], moved), right)
    out = both[:, :PAIR] + both[:, PAIR:]
    blank = jnp.zeros((size, PAIR), F32)
    return rows(*[part for c in cuts for part in (blank, out[c // 2 : c // 2 + size])])


def advance(summary, state):
    pad = jnp.zeros((WIDTH, PAIR), F32)
    lane = lax.broadcasted_iota(jnp.int32, (WIDTH, PAIR), 1)
    moved = product(halves(summary), halves(rows(pad, state)))
    return moved + jnp.where(lane < WIDTH, summary, 0.0)


def side_by_side(ref, head):
    return lanes(ref[pl.ds(head, 1), :], ref[pl.ds(head + 1, 1), :])


def same_head():
    row = lax.broadcasted_iota(jnp.int32, (2 * PAIR, PAIR), 0)
    col = lax.broadcasted_iota(jnp.int32, (2 * PAIR, PAIR), 1)
    return jnp.where((row // WIDTH) % 2 == col // WIDTH, 1.0, 0.0).astype(BF16)


def scores_of(left, right, h):
    keep = (lax.broadcasted_iota(jnp.int32, right[0].shape, 1) < WIDTH) == (h == 0)
    high, low = [jnp.where(keep, part, jnp.zeros((), BF16)) for part in right]
    return dot_nt(lanes(*left), lanes(high, high)) + dot_nt(left[0], low)


def local_step(
    places, w_ref, k_ref, v_ref, a_ref, factor_ref, w_ready, ready,
    shifts, cums, maps, sums, rights, keys, summ, masks,
):
    tokens = k_ref.shape[0]
    half = tokens // 2
    row = lax.broadcasted_iota(jnp.int32, (tokens, tokens), 0)
    col = lax.broadcasted_iota(jnp.int32, (tokens, tokens), 1)
    strict = row > col
    lane = lax.broadcasted_iota(jnp.int32, (tokens, PAIR), 1)
    first = lane < WIDTH
    signs = jnp.where(
        (row >= col) & (col >= half), 1.0, jnp.where((row < col) & (col < half), -1.0, 0.0)
    ).astype(BF16)
    same = same_head()
    srow = lax.broadcasted_iota(jnp.int32, (WIDTH, PAIR), 0)
    slane = lax.broadcasted_iota(jnp.int32, (WIDTH, PAIR), 1)
    diagonal = srow == slane % WIDTH
    sfirst = slane < WIDTH
    zero = jnp.zeros((), F32)

    pairs = range(len(places))
    spans = [pl.ds(pl.multiple_of(place * PAIR, PAIR), PAIR) for place in places]
    w_ready()
    decays = []
    for p in pairs:
        at = spans[p]
        log_w = w_ref[:, at]
        cum = sum(dot(signs, part) for part in reversed(thirds(log_w)))
        cums[:, at] = cum
        start = cum[0:1] - log_w[0:1]
        last = cum[tokens - 1 : tokens]
        shift = jnp.exp(-start)
        shifts[pl.ds(places[p], 1), :] = shift
        decays.append(
            (jnp.exp(cum - log_w), jnp.exp(-cum), jnp.exp(last), jnp.exp(last - start), shift)
        )
    ready()
    prepared = []
    for p in pairs:
        at = spans[p]
        k = k_ref[:, at].astype(F32)
        v = v_ref[:, at]
        a = a_ref[:, at].astype(F32)
        ahead, grow, to_end, whole, shift = decays[p]
        removal = k * side_by_side(factor_ref, 2 * places[p])
        square = dot(lanes(*halves(removal * removal)), same)
        kappa = removal * lax.rsqrt(square + 1e-06 * WIDTH)
        b = a * kappa
        kappa_mid = kappa * ahead
        k_mid = k * grow
        b_mid = b * grow
        left = halves(kappa_mid)
        right = halves(rows(b_mid, k_mid))
        keys[places[p]] = lanes(*right)
        ends = halves(jnp.transpose(lanes(k_mid * to_end, b_mid * -to_end)))
        swapped = pltpu.roll(kappa_mid * shift, WIDTH, 1)
        whole = pltpu.roll(jnp.broadcast_to(whole, (WIDTH, PAIR)), WIDTH, 1)
        prepared.append((v, left, right, ends, swapped, whole))

    heads = [(p, h) for p in pairs for h in range(2)]
    scores = [scores_of(prepared[p][1], prepared[p][2], h) for p, h in heads]
    lower = [jnp.where(strict, s[:, :tokens], zero) for s in scores]
    mix_key = [halves(jnp.where(strict, s[:, tokens:], zero)) for s in scores]
    values, wanted = [], []
    for i, (p, h) in enumerate(heads):
        v, swapped = prepared[p][0], prepared[p][4]
        mine = first == (h == 0)
        own_v = jnp.where(mine, v, jnp.zeros((), BF16))
        values.append(own_v)
        pushed = dot(lanes(*mix_key[i]), rows(own_v, own_v))
        wanted.append(pushed + jnp.where(mine, zero, swapped))

    yield

    lower = [halves(l) for l in lower]
    eye = jnp.where(row == col, 1.0, 0.0).astype(BF16)
    inverse = [(eye - high * masks[0], -low * masks[0]) for high, low in lower]
    size, level = 2, 1
    while size < tokens:
        mask = masks[level]
        edge = [(high * mask, low * mask) for high, low in lower]
        step = [below_left(e, m, size, 0) for e, m in zip(edge, inverse)]
        step = [below_left(m, halves(s), size, 1) for m, s in zip(inverse, step)]
        step = [halves(s) for s in step]
        inverse = [(m[0] - s[0], m[1] - s[1]) for m, s in zip(inverse, step)]
        size, level = 2 * size, level + 1

    removed = [halves(product(m, halves(w))) for m, w in zip(inverse, wanted)]
    outs = []
    for i, (p, h) in enumerate(heads):
        ends = prepared[p][3]
        cut = slice(h * WIDTH, (h + 1) * WIDTH)
        stack = rows(
            *[lanes(e[cut, :], e[PAIR + h * WIDTH : PAIR + (h + 1) * WIDTH, :]) for e in ends]
        )
        right = rows(lanes(values[i], jnp.zeros_like(values[i])), lanes(*removed[i]))
        rights[2 * places[p] + h] = right
        both = dot(stack, right)
        both = both[:, :PAIR] + both[:, PAIR:]
        outs.append(both[:WIDTH] + both[WIDTH:])
    for p in pairs:
        fade = jnp.where(diagonal, prepared[p][5], zero)
        one = outs[2 * p] + jnp.where(sfirst, zero, fade)
        two = outs[2 * p + 1] + jnp.where(sfirst, fade, zero)
        summ[0, places[p]] = one
        summ[1, places[p]] = pltpu.roll(two, WIDTH, 1)
        maps[places[p]] = jnp.where(sfirst, two, one)
        sums[places[p]] = jnp.where(sfirst, one, two)


def read_step(group, count, r_ref, k_ref, v_ref, gain_ref, shifts, cums, own, reach, rights, keys):
    tokens = own.shape[0]
    row = lax.broadcasted_iota(jnp.int32, (tokens, 2 * tokens), 0)
    col = lax.broadcasted_iota(jnp.int32, (tokens, 2 * tokens), 1)
    incl = row >= col % tokens
    first = lax.broadcasted_iota(jnp.int32, (tokens, PAIR), 1) < WIDTH
    same = same_head()
    prepared = []
    for p in range(count):
        pair = group * count + p
        at = pl.ds(pl.multiple_of(pair * PAIR, PAIR), PAIR)
        r = r_ref[:, at].astype(F32)
        r_mid = r * jnp.exp(cums[:, at])
        gained = r * side_by_side(gain_ref, 2 * pair) * k_ref[:, at].astype(F32)
        bonus = dot(lanes(*halves(gained)), same)
        key = keys[pair]
        prepared.append(
            (
                at,
                halves(r_mid),
                (key[:, :PAIR], key[:, PAIR:]),
                bonus * v_ref[:, at].astype(F32),
                pltpu.roll(r_mid * shifts[pl.ds(pair, 1), :], WIDTH, 1),
            )
        )
    reads = []
    for at, left, right, _, _ in prepared:
        for h in range(2):
            score = scores_of(left, right, h)
            score = lanes(score[:, tokens:], -score[:, :tokens])
            reads.append(rows(*halves(jnp.where(incl, score, 0.0))))
    outs = []
    for i, read in enumerate(reads):
        both = dot(read, rights[group * 2 * count + i])
        both = both[:, :PAIR] + both[:, PAIR:]
        outs.append(both[:tokens] + both[tokens:])
    for p, (at, _, _, bonus, entry) in enumerate(prepared):
        one, two = outs[2 * p], outs[2 * p + 1]
        own[:, at] = bonus + jnp.where(first, one, two)
        reach[:, at] = entry + jnp.where(first, two, one)


def fold_step(pair, own, reach, maps, sums, first, second):
    tokens = own.shape[0]
    low = lax.broadcasted_iota(jnp.int32, (WIDTH, PAIR), 1) < WIDTH
    at = pl.ds(pl.multiple_of(pair * PAIR, PAIR), PAIR)
    one, two = first[pair], pltpu.roll(second[pair], WIDTH, 1)
    right = rows(
        lanes(jnp.where(low, two, 0.0), jnp.where(low, 0.0, two)),
        lanes(jnp.where(low, 0.0, one), jnp.where(low, one, 0.0)),
    )
    high, rest = halves(right)
    left = halves(rows(reach[:, at], maps[pair]))
    moved = dot(lanes(*left), rows(high, high)) + dot(left[0], rest)
    reach[:, at] = moved[:tokens, :PAIR]
    own[:, at] += moved[:tokens, PAIR:]
    maps[pair] = moved[tokens:, :PAIR]
    sums[pair] += moved[tokens:, PAIR:]


def enter_step(pair, own, reach, maps, sums, inbox, out_ref, state_ref):
    tokens = own.shape[0]
    zero = jnp.zeros((WIDTH, WIDTH), F32)
    at = pl.ds(pl.multiple_of(pair * PAIR, PAIR), PAIR)
    one, two = [
        rows(inbox[h, pair][:, :WIDTH], inbox[h, pair][:, WIDTH:]) for h in range(2)
    ]
    entry = halves(rows(lanes(zero, two), lanes(one, zero)))
    moved = product(halves(rows(reach[:, at], maps[pair])), entry)
    out_ref[:, at] = own[:, at] + moved[:tokens]
    after = sums[pair] + moved[tokens:]
    state_ref[0, 2 * pair] = after[:, :WIDTH]
    state_ref[0, 2 * pair + 1] = after[:, WIDTH:]


def kernel(
    chains, chips, r_in, k_in, v_in, w_in, a_in, factor_in, gain_in, out_ref, state_ref,
    r_ref, k_ref, v_ref, w_ref, a_ref, factor_ref, gain_ref, load, shifts, cums,
    own, reach, maps, sums, rights, keys, summ, masks, both, other, joined, parts, starts, totals,
    inbox, outbox, send_m, recv_m, send_a, recv_a, send_b, recv_b, send_c, recv_c, send_f, recv_f,
):
    sources = (w_in, k_in, factor_in, a_in, v_in, r_in, gain_in)
    targets = (w_ref, k_ref, factor_ref, a_ref, v_ref, r_ref, gain_ref)
    loads = [
        pltpu.make_async_copy(source, target, load.at[i])
        for i, (source, target) in enumerate(zip(sources, targets))
    ]
    for copy in loads:
        copy.start()
    chain = lax.axis_index("chain")
    seq = lax.axis_index("seq")
    core = lax.rem(seq, 2)
    chip = seq // 2
    partner = {"seq": seq + 1 - 2 * core}
    barrier = pltpu.get_barrier_semaphore()
    ways = sorted(range(1, chips), key=lambda way: -min(way, chips - way))

    def there(way):
        return lax.rem(chip + way, chips)

    def device(way):
        return {"seq": 2 * there(way) + core}

    def greet(device_id):
        pl.semaphore_signal(barrier, inc=1, device_id=device_id, device_id_type=MESH)

    totals[...] = jnp.zeros_like(totals)
    greet(partner)
    for way in ways:
        greet(device(way))
    for step in range(1, chains):
        greet({"chain": lax.rem(chain + step, chains)})
    row = lax.broadcasted_iota(jnp.int32, masks.shape[1:], 0)
    col = lax.broadcasted_iota(jnp.int32, masks.shape[1:], 1)
    for level in range(masks.shape[0]):
        size = 1 << level
        inside = (row // (2 * size) == col // (2 * size)) & (row // size > col // size)
        masks[level] = jnp.where(inside, 1.0, 0.0).astype(BF16)

    def ready():
        for copy in loads[1:]:
            copy.wait()

    order = ways + [0]
    half = chips // 2 + (1 if chips > 2 else 0)

    def local(ways_of, w_ready, ready):
        return local_step(
            [there(way) for way in ways_of], w_ref, k_ref, v_ref, a_ref, factor_ref,
            w_ready, ready, shifts, cums, maps, sums, rights, keys, summ, masks,
        )

    def swap(way):
        return pltpu.make_async_remote_copy(
            src_ref=summ.at[1 - core, there(way)],
            dst_ref=both.at[core, there(way)],
            send_sem=send_m.at[way],
            recv_sem=recv_m.at[way],
            device_id=partner,
            device_id_type=MESH,
        )

    swap_rest = pltpu.make_async_remote_copy(
        src_ref=summ.at[0],
        dst_ref=other,
        send_sem=send_m.at[chips],
        recv_sem=recv_m.at[chips],
        device_id=partner,
        device_id_type=MESH,
    )
    def gather(way):
        return pltpu.make_async_remote_copy(
            src_ref=joined.at[there(way)],
            dst_ref=parts.at[chip],
            send_sem=send_a.at[way],
            recv_sem=recv_a.at[chips - way],
            device_id=device(way),
            device_id_type=MESH,
        )

    def offer(ways_of):
        for way in ways_of:
            swap(way).start()
        for way in ways_of:
            both[core, there(way)] = summ[core, there(way)]

    def join(ways_of):
        for way in ways_of:
            swap(way).wait_recv()
        made = [advance(both[1, there(way)], both[0, there(way)]) for way in ways_of]
        for way, summary in zip(ways_of, made):
            joined[there(way)] = summary
        for way in ways_of:
            if way:
                gather(way).start()

    for _ in local(order[:half], loads[0].wait, ready):
        pass
    pl.semaphore_wait(barrier, chips + chains - 1)
    offer(order[:half])
    rest = local(order[half:], lambda: None, lambda: None)
    next(rest)
    join(order[:half])
    for _ in rest:
        pass
    offer(order[half:])

    @pl.when(core == 0)
    def _():
        swap_rest.start()

    for at in range(half, chips, 2):
        join(order[at : min(at + 2, chips)])
    parts[chip] = joined[chip]

    count = min(2, chips)

    def read(group, _):
        read_step(
            group, count, r_ref, k_ref, v_ref, gain_ref, shifts, cums, own, reach, rights, keys
        )
        return 0

    groups = chips // count
    early = groups * 2 // 4
    lax.fori_loop(0, early, read, 0)

    for way in ways:
        gather(way).wait_recv()

    levels = [[parts[place] for place in range(chips)]]
    while len(levels[-1]) > 1:
        below = levels[-1]
        levels.append([advance(below[i + 1], below[i]) for i in range(0, len(below), 2)])
    totals[chain] = levels[-1][0]

    def pass_on(step):
        return pltpu.make_async_remote_copy(
            src_ref=totals.at[chain],
            dst_ref=totals.at[chain],
            send_sem=send_b.at[step],
            recv_sem=recv_b.at[step],
            device_id={"chain": lax.rem(chain + step, chains)},
            device_id_type=MESH,
        )

    def take(step):
        return pltpu.make_async_remote_copy(
            src_ref=totals.at[chain],
            dst_ref=totals.at[lax.rem(chain - step + chains, chains)],
            send_sem=send_b.at[step],
            recv_sem=recv_b.at[step],
            device_id={"chain": lax.rem(chain + step, chains)},
            device_id_type=MESH,
        )

    for step in range(chains - 1, 0, -1):

        @pl.when(chain + step < chains)
        def _():
            pass_on(step).start()

    row = lax.broadcasted_iota(jnp.int32, (WIDTH, PAIR), 0)
    lane = lax.broadcasted_iota(jnp.int32, (WIDTH, PAIR), 1)
    before = [None]
    for level in reversed(levels[:-1]):
        spread = []
        for i, state in enumerate(before):
            here = level[2 * i]
            spread += [state, here if state is None else advance(here, state)]
        before = spread
    before[0] = jnp.where(lane == row + WIDTH, 1.0, 0.0)
    for place in range(chips):
        starts[place] = before[place]

    lax.fori_loop(early, groups, read, 0)

    for step in range(1, chains):

        @pl.when(chain >= step)
        def _():
            take(step).wait_recv()

    state = jnp.where(chain > 0, totals[0], 0.0)
    for place in range(1, chains - 1):
        state = jnp.where(place < chain, advance(totals[place], state), state)
    state = jnp.where(lane < WIDTH, state, 0.0)

    entry = halves(rows(jnp.zeros((WIDTH, PAIR), F32), state))
    for place in range(chips):
        moved = product(halves(starts[place]), entry) + starts[place]
        outbox[place] = lanes(moved[: WIDTH // 2, :WIDTH], moved[WIDTH // 2 :, :WIDTH])

    def reply(way):
        return pltpu.make_async_remote_copy(
            src_ref=outbox.at[there(way)],
            dst_ref=inbox.at[core, chip],
            send_sem=send_c.at[way],
            recv_sem=recv_c.at[chips - way],
            device_id=device(way),
            device_id_type=MESH,
        )

    def hand_on(way):
        return pltpu.make_async_remote_copy(
            src_ref=inbox.at[core, there(way)],
            dst_ref=inbox.at[core, there(way)],
            send_sem=send_f.at[way],
            recv_sem=recv_f.at[way],
            device_id=partner,
            device_id_type=MESH,
        )

    def handed(way):
        return pltpu.make_async_remote_copy(
            src_ref=inbox.at[core, there(way)],
            dst_ref=inbox.at[1 - core, there(way)],
            send_sem=send_f.at[way],
            recv_sem=recv_f.at[way],
            device_id=partner,
            device_id_type=MESH,
        )

    for way in ways:
        reply(way).start()
    inbox[core, chip] = outbox[chip]
    hand_on(0).start()

    @pl.when(core == 1)
    def _():
        swap_rest.wait_recv()

        def fold(pair, _):
            fold_step(pair, own, reach, maps, sums, other, both.at[0])
            return 0

        lax.fori_loop(0, chips, fold, 0)

    turn = [0] + ways[::-1]
    for way in turn[1:]:
        reply(chips - way).wait_recv()
        hand_on(way).start()
    for at in range(0, chips, 4):
        for way in turn[at : at + 4]:
            handed(way).wait_recv()
        for way in turn[at : at + 4]:
            enter_step(there(way), own, reach, maps, sums, inbox, out_ref, state_ref)

    for way in order:
        swap(way).wait_send()

    @pl.when(core == 0)
    def _():
        swap_rest.wait_send()

    for way in ways:
        gather(way).wait_send()
        reply(way).wait_send()
    for way in [0] + ways:
        hand_on(way).wait_send()
    for step in range(1, chains):

        @pl.when(chain + step < chains)
        def _():
            pass_on(step).wait_send()


def deliver_kernel(out_ref, state_ref, out_hbm, state_hbm, sems):
    copies = [
        pltpu.make_async_copy(out_ref, out_hbm, sems.at[0]),
        pltpu.make_async_copy(state_ref, state_hbm, sems.at[1]),
    ]
    for copy in copies:
        copy.start()
    for copy in copies:
        copy.wait()


def deliver(*results):
    return pl.pallas_call(
        deliver_kernel,
        in_specs=[pl.BlockSpec(memory_space=pltpu.VMEM)] * 2,
        out_specs=[pl.BlockSpec(memory_space=pltpu.HBM)] * 2,
        out_shape=[jax.ShapeDtypeStruct(x.shape, x.dtype) for x in results],
        scratch_shapes=[pltpu.SemaphoreType.DMA((2,))],
        compiler_params=pltpu.CompilerParams(vmem_limit_bytes=VMEM_LIMIT),
        name="deliver",
    )(*results)


def solution(mesh):
    chains, chips = mesh.shape["chain"], mesh.shape["seq"] // 2

    def body(*args):
        tokens, columns = args[0].shape
        heads = columns // WIDTH
        half = WIDTH // 2
        vmem = pl.BlockSpec(memory_space=pltpu.VMEM)
        each = pltpu.VMEM((chips, WIDTH, PAIR), F32)
        sems = pltpu.SemaphoreType.DMA
        results = pl.pallas_call(
            functools.partial(kernel, chains, chips),
            in_specs=[pl.BlockSpec(memory_space=pltpu.HBM)] * 7,
            out_specs=[vmem] * 2,
            out_shape=[
                jax.ShapeDtypeStruct((tokens, columns), F32),
                jax.ShapeDtypeStruct((1, heads, WIDTH, WIDTH), F32),
            ],
            scratch_shapes=[
                pltpu.VMEM((tokens, columns), BF16),
                pltpu.VMEM((tokens, columns), BF16),
                pltpu.VMEM((tokens, columns), BF16),
                pltpu.VMEM((tokens, columns), F32),
                pltpu.VMEM((tokens, columns), BF16),
                pltpu.VMEM((heads, WIDTH), F32),
                pltpu.VMEM((heads, WIDTH), F32),
                sems((7,)),
                pltpu.VMEM((chips, PAIR), F32),
                pltpu.VMEM((tokens, columns), F32),
                pltpu.VMEM((tokens, columns), F32),
                pltpu.VMEM((tokens, columns), F32),
                each,
                each,
                pltpu.VMEM((heads, 2 * tokens, 2 * PAIR), BF16),
                pltpu.VMEM((chips, 2 * tokens, 2 * PAIR), BF16),
                pltpu.VMEM((2, chips, WIDTH, PAIR), F32),
                pltpu.VMEM((7, tokens, tokens), BF16),
                pltpu.VMEM((2, chips, WIDTH, PAIR), F32),
                each,
                each,
                each,
                each,
                pltpu.VMEM((chains, WIDTH, PAIR), F32),
                pltpu.VMEM((2, chips, half, PAIR), F32),
                pltpu.VMEM((chips, half, PAIR), F32),
                sems((chips + 1,)), sems((chips + 1,)), sems((chips,)), sems((chips,)),
                sems((chains,)), sems((chains,)), sems((chips,)), sems((chips,)), sems((chips,)), sems((chips,)),
            ],
            compiler_params=pltpu.CompilerParams(
                collective_id=0, has_side_effects=True, vmem_limit_bytes=VMEM_LIMIT
            ),
            name="mix",
        )(*[pltpu.with_memory_space_constraint(x, pltpu.HBM) for x in args])
        return deliver(*results)

    wide = P(("chain", "seq"), "head")
    return jax.shard_map(
        body,
        mesh=mesh,
        in_specs=(wide,) * 5 + (P("head", None),) * 2,
        out_specs=(wide, P(("chain", "seq"), "head", None, None)),
        check_vma=False,
    )
```
